512 devices in a mesh: panel: 32 (over x_hi, y, core), row: 16 (over z, x_lo).
Axes of the slice: x: 4 (x_hi: 2, x_lo: 2; x = x_hi * 2 + x_lo), y: 8, z: 8, core: 2. Of those that a mesh axis runs over, the one named last changes fastest.
Arguments:
- slab: float32 [16384, 8192], P('row', 'panel'), may hold values from -6 to 6
- boundary: float32 [16384, 256], P('row'), may hold values from -6 to 6
- diag_inverse: float32 [8192, 256], P(('panel', 'row')), may hold values from -1 to 1.6, as said below
- sub_block: float32 [8192, 256], P(('panel', 'row')), may hold values from -0.375 to 0.375
- tail_coupling: float32 [8192, 256], P(('panel', 'row')), may hold values from -0.0625 to 0.0625
- tail_cols: float32 [16384, 256], P(('row', 'panel')), may hold values from -6 to 6
Outputs:
- factor: float32 [16384, 8192], P('row', 'panel')
- tail_out: float32 [16384, 256], P(('row', 'panel'))
The draws below stay inside these ranges and needn't reach their ends.
Inputs may be any that keep to these rules, and one draw needn't show every extreme that they name: `diag_inverse`: each block of 256 rows is lower triangular with a positive diagonal of 0.6 to 1.6.
All inputs are finite; a program needn't handle non-finite values.
Results may differ from the reference program's by a relative error of at most 0.00029.
Values sent between devices are 32-bit elements; how exact they have to be, the bound alone decides.
A program may use at most 128 MiB of HBM per device.

```python
import math
import jax
import jax.numpy as jnp
from jax import lax

B = 256
PANELS = 32
ROWS = 16384


def draw_diag_inverse(key, part):
    key_diag, key_off = jax.random.split(jax.random.fold_in(key, 17))
    total = PANELS * B
    within = (jnp.arange(total) % B)[:, None]
    column = jnp.arange(B)[None, :]
    diagonal = jnp.exp(jax.random.uniform(key_diag, (total, 1), jnp.float32, math.log(0.7), math.log(1.4)))
    offdiag = jnp.clip(jax.random.normal(key_off, (total, B), jnp.float32), -4.0, 4.0) * (0.3 / math.sqrt(B))
    return jnp.where(column == within, diagonal, jnp.where(column < within, offdiag, 0.0)).astype(jnp.float32)


def shard_levels(own_key, dims, shards, smallest, high):
    def one(axis_at, shards_of):
        heights = jax.random.uniform(jax.random.fold_in(jax.random.fold_in(own_key, 6), axis_at), (shards_of,), jnp.float32, smallest / len(shards), high / len(shards))
        return jnp.repeat(jnp.exp(heights), dims[axis_at] // shards_of).reshape((-1,) + (1,) * (len(dims) - axis_at - 1))

    level = one(*shards[0])
    for cut in shards[1:]:
        level = level * one(*cut)
    return level


def centred(own_key, extent, deviation, most, cuts=(), dtype=jnp.bfloat16):
    entries = jax.random.normal(own_key, extent, jnp.float32) * deviation
    if len(cuts) > 0:
        entries = shard_levels(own_key, extent, cuts, -0.22, 0.18) * entries
    return jnp.clip(entries, min=-most, max=most).astype(dtype)


def setup_inputs(seed: int = 0) -> dict:
    streams_of = jax.random.split(jax.random.key(seed), 7)
    slab = centred(streams_of[0], (ROWS, PANELS * B), 1.0, 6.0, ((0, 16), (1, 32)), jnp.float32)
    boundary = centred(streams_of[1], (ROWS, B), 1.0, 6.0, ((0, 16),), jnp.float32)
    diag_inverse = draw_diag_inverse(jax.random.fold_in(streams_of[6], 71), 0)
    sub_block = centred(streams_of[3], (PANELS * B, B), (B + B // 10) ** -0.5, 0.375, ((0, 512),), jnp.float32)
    tail_coupling = centred(streams_of[4], (PANELS * B, B), (B * PANELS) ** -0.5, 0.0625, ((0, 512),), jnp.float32)
    tail_cols = centred(streams_of[5], (ROWS, B), 1.0, 6.0, ((0, 512),), jnp.float32)
    return {"slab": slab, "boundary": boundary, "diag_inverse": diag_inverse, "sub_block": sub_block, "tail_coupling": tail_coupling, "tail_cols": tail_cols}


def transpose_dot(left, right):
    return lax.dot_general(left, right, (((1,), (1,)), ((), ())), precision=lax.Precision.HIGHEST, preferred_element_type=jnp.float32)


def reference(slab, boundary, diag_inverse, sub_block, tail_coupling, tail_cols):
    previous = boundary
    pieces = []
    summed = jnp.zeros((slab.shape[0], B), jnp.float32)
    for panel_index in range(PANELS):
        low = panel_index * B
        inverse = diag_inverse[low:low + B]
        beneath = sub_block[low:low + B]
        coupling = tail_coupling[low:low + B]
        solved = transpose_dot(slab[:, low:low + B] - transpose_dot(previous, beneath), inverse)
        summed = summed + jnp.dot(solved, coupling, precision=lax.Precision.HIGHEST, preferred_element_type=jnp.float32)
        pieces.append(solved)
        previous = solved
    return jnp.concatenate(pieces, axis=1), tail_cols - summed
```

```python
import functools

import jax
import jax.numpy as jnp
from jax import lax
from jax.experimental import pallas as pl
from jax.experimental.pallas import tpu as pltpu
from jax.sharding import PartitionSpec as P

MESH = pl.DeviceIdType.MESH
BATCH = 32
NT = (((1,), (1,)), ((), ()))
NN = (((1,), (0,)), ((), ()))


def split(value):
    high = value.astype(jnp.bfloat16)
    low = (value - high.astype(jnp.float32)).astype(jnp.bfloat16)
    return high, low


def dot3(left, right, dims):
    left_high, left_low = split(left)
    right_high, right_low = split(right)
    dot = functools.partial(lax.dot_general, dimension_numbers=dims, preferred_element_type=jnp.float32)
    return dot(left_high, right_high) + (dot(left_high, right_low) + dot(left_low, right_high))


def kernel(
    panels, rows,
    slab, boundary, inverse_ref, beneath_ref, coupling_ref, cols_ref,
    factor_ref, tail_ref,
    slabs, inverses, beneath, couplings, products, constants, step_high, step_low,
    offset, entering, solved, share, sums_in, sums_out, total,
    z_send, z_recv, x_send, x_recv, pair_send, pair_recv, local_sem,
    y_send, y_recv, s_send, s_recv, t_send, t_recv,
):
    p, r = lax.axis_index("panel"), lax.axis_index("row")
    core = lax.rem(p, 2)
    chip = lax.div(p, 2)
    chips = panels // 2
    z, x = lax.div(r, 2), lax.rem(r, 2)
    depth = rows // 2
    half = slab.shape[0] // 2
    nbatch = half // BATCH
    width = slab.shape[1]
    mine = pl.ds(pl.multiple_of(core * half, half), half)
    other = pl.ds(pl.multiple_of((1 - core) * half, half), half)
    sibling = {"panel": p + 1 - 2 * core, "row": r}
    beside = {"panel": p, "row": r + 1 - 2 * x}
    after = {"panel": p + 2, "row": r}
    ahead = {"panel": p - 2, "row": r}
    collector = {"panel": panels - 2 + lax.div(p, panels // 2), "row": r}
    steps = sorted(range(1, depth), key=lambda d: (min(d, depth - d), d))

    def z_row(shift):
        return lax.rem(z + shift + depth, depth) * 2 + x

    local_slab = pltpu.make_async_copy(slab.at[mine], slabs.at[core], local_sem.at[0])
    local_slab.start()

    barrier = pltpu.get_barrier_semaphore()

    def greet(target):
        pl.semaphore_signal(barrier, inc=1, device_id=target, device_id_type=MESH)

    for shift in steps:
        greet({"panel": p, "row": z_row(shift)})
    greet(beside)
    greet(sibling)
    last = chip == chips - 1

    @pl.when(chip > 0)
    def _():
        greet(ahead)

    @pl.when(p < panels - 1)
    def _():
        greet(collector)

    gathering = jnp.where(last, panels // 2 - core, 1)
    pl.semaphore_wait(barrier, depth + 1 + gathering)

    full = (inverses.at[core], beneath, couplings.at[core])
    shards = (inverse_ref, beneath_ref, coupling_ref)

    def z_copy(k, i, shift):
        return pltpu.make_async_remote_copy(
            src_ref=shards[k], dst_ref=full[k].at[r], send_sem=z_send.at[k, i], recv_sem=z_recv.at[k, i],
            device_id={"panel": p, "row": z_row(shift)}, device_id_type=MESH,
        )

    def z_arrival(k, i, shift):
        return pltpu.make_async_remote_copy(
            src_ref=shards[k], dst_ref=full[k].at[z_row(-shift)], send_sem=z_send.at[k, i], recv_sem=z_recv.at[k, i],
            device_id={"panel": p, "row": z_row(shift)}, device_id_type=MESH,
        )

    def x_own(k):
        return pltpu.make_async_remote_copy(
            src_ref=shards[k], dst_ref=full[k].at[r], send_sem=x_send.at[k, depth - 1], recv_sem=x_recv.at[k, depth - 1],
            device_id=beside, device_id_type=MESH,
        )

    def x_relay(k, i, shift):
        place = full[k].at[z_row(-shift)]
        return pltpu.make_async_remote_copy(
            src_ref=place, dst_ref=place, send_sem=x_send.at[k, i], recv_sem=x_recv.at[k, i],
            device_id=beside, device_id_type=MESH,
        )

    def x_arrivals(k):
        x_own(k).wait_recv()
        for i, shift in enumerate(steps):
            x_relay(k, i, shift).wait_recv()

    def to_sibling(k, src, dst):
        return pltpu.make_async_remote_copy(
            src_ref=src, dst_ref=dst, send_sem=pair_send.at[k], recv_sem=pair_recv.at[k],
            device_id=sibling, device_id_type=MESH,
        )

    pair_slab = to_sibling(0, slab.at[other], slabs.at[core])
    pair_inverse = to_sibling(1, inverses.at[core], inverses.at[core])
    pair_product = to_sibling(2, products.at[core], products.at[core])
    pair_coupling = to_sibling(3, couplings.at[core], couplings.at[core])
    pair_factor = to_sibling(4, solved.at[1 - core], factor_ref.at[mine])

    for k in range(3):
        x_own(k).start()
        for i, shift in enumerate(steps):
            z_copy(k, i, shift).start()
        if k == 0:
            pair_slab.start()
    for k in range(3):
        full[k][r] = shards[k][...]

    def relay(k):
        for i, shift in enumerate(steps):
            z_arrival(k, i, shift).wait_recv()
            x_relay(k, i, shift).start()

    def square(ref):
        return ref[...].reshape(width, width)

    relay(0)
    relay(1)
    x_arrivals(0)
    pair_inverse.start()
    x_arrivals(1)
    products[core] = dot3(square(inverses.at[core]), square(beneath), NN)
    pair_product.start()
    local_slab.wait()
    constants[core] = dot3(slabs[core], square(inverses.at[core]), NT)
    pair_slab.wait_recv()
    pair_inverse.wait_recv()
    constants[1 - core] = dot3(slabs[1 - core], square(inverses.at[1 - core]), NT)
    pair_product.wait_recv()
    step_high[...], step_low[...] = split(dot3(products[1], products[0], NN).T)
    offset[...] = constants[1] - dot3(constants[0], products[1], NT)

    @pl.when(chip == 0)
    def _():
        load = pltpu.make_async_copy(boundary.at[mine], entering, local_sem.at[1])
        load.start()
        load.wait()

    def batch(b):
        return pl.ds(pl.multiple_of(b * BATCH, BATCH), BATCH)

    def y_copy(b):
        return pltpu.make_async_remote_copy(
            src_ref=solved.at[1, batch(b)], dst_ref=entering.at[batch(b)], send_sem=y_send.at[b], recv_sem=y_recv.at[b],
            device_id=after, device_id_type=MESH,
        )

    def advance(b, carry):
        @pl.when(chip > 0)
        def _():
            y_copy(b).wait_recv()

        high, low = split(entering[batch(b)])
        both = jnp.dot(jnp.concatenate([high, low], axis=0), step_high[...], preferred_element_type=jnp.float32)
        rest = jnp.dot(high, step_low[...], preferred_element_type=jnp.float32)
        solved[1, batch(b)] = offset[batch(b)] + (both[:BATCH] + (both[BATCH:] + rest))

        @pl.when(chip < chips - 1)
        def _():
            y_copy(b).start()

        return carry

    lax.fori_loop(0, nbatch // 2, advance, 0)
    relay(2)
    lax.fori_loop(nbatch // 2, nbatch, advance, 0)
    x_arrivals(2)
    pair_coupling.start()
    solved[0] = constants[0] - dot3(entering[...], products[0], NT)
    pair_factor.start()
    share[...] = dot3(solved[core], square(couplings.at[core]), NN)
    factor_ref[mine] = solved[core]
    pair_coupling.wait_recv()
    share[...] += dot3(solved[1 - core], square(couplings.at[1 - core]), NN)

    def s_copy(b):
        return pltpu.make_async_remote_copy(
            src_ref=sums_out.at[batch(b)], dst_ref=sums_in.at[batch(b)], send_sem=s_send.at[b], recv_sem=s_recv.at[b],
            device_id=after, device_id_type=MESH,
        )

    def t_copy(b):
        return pltpu.make_async_remote_copy(
            src_ref=sums_out.at[batch(b)], dst_ref=total, send_sem=t_send.at[b], recv_sem=t_recv.at[0],
            device_id={"panel": core * nbatch + b, "row": r}, device_id_type=MESH,
        )

    def add_up(b, carry):
        @pl.when(chip == 0)
        def _():
            sums_out[batch(b)] = share[batch(b)]

        @pl.when(chip > 0)
        def _():
            s_copy(b).wait_recv()
            sums_out[batch(b)] = sums_in[batch(b)] + share[batch(b)]

        @pl.when(chip < chips - 1)
        def _():
            s_copy(b).start()

        owner = core * nbatch + b

        @pl.when(last & (owner != p))
        def _():
            t_copy(b).start()

        @pl.when(last & (owner == p))
        def _():
            total[...] = sums_out[batch(b)]

        return carry

    lax.fori_loop(0, nbatch, add_up, 0)

    @pl.when(p < panels - 1)
    def _():
        t_copy(0).wait_recv()

    tail_ref[...] = cols_ref[...] - total[...]

    def drain(b, carry):
        @pl.when(chip < chips - 1)
        def _():
            y_copy(b).wait_send()
            s_copy(b).wait_send()

        @pl.when(last & (core * nbatch + b != p))
        def _():
            t_copy(b).wait_send()

        return carry

    lax.fori_loop(0, nbatch, drain, 0)
    for k in range(3):
        x_own(k).wait_send()
        for i, shift in enumerate(steps):
            z_copy(k, i, shift).wait_send()
            x_relay(k, i, shift).wait_send()
    pair_slab.wait_send()
    pair_inverse.wait_send()
    pair_product.wait_send()
    pair_coupling.wait_send()
    pair_factor.wait()


def solution(mesh):
    panels, rows = mesh.shape["panel"], mesh.shape["row"]

    def on_device(slab, boundary, diag_inverse, sub_block, tail_coupling, tail_cols):
        height, width = slab.shape
        half = height // 2
        depth = rows // 2
        nbatch = half // BATCH
        f32 = jnp.float32
        shard = diag_inverse.shape[0]
        whole = pl.BlockSpec(memory_space=pltpu.VMEM)
        apart = pl.BlockSpec(memory_space=pl.ANY)
        dma = pltpu.SemaphoreType.DMA
        return pl.pallas_call(
            functools.partial(kernel, panels, rows),
            out_shape=(
                jax.ShapeDtypeStruct((height, width), f32),
                jax.ShapeDtypeStruct(tail_cols.shape, f32),
            ),
            in_specs=[apart, apart, whole, whole, whole, whole],
            out_specs=(whole, whole),
            scratch_shapes=[
                pltpu.VMEM((2, half, width), f32),
                pltpu.VMEM((2, rows, shard, width), f32),
                pltpu.VMEM((rows, shard, width), f32),
                pltpu.VMEM((2, rows, shard, width), f32),
                pltpu.VMEM((2, width, width), f32),
                pltpu.VMEM((2, half, width), f32),
                pltpu.VMEM((width, width), jnp.bfloat16),
                pltpu.VMEM((width, width), jnp.bfloat16),
                pltpu.VMEM((half, width), f32),
                pltpu.VMEM((half, width), f32),
                pltpu.VMEM((2, half, width), f32),
                pltpu.VMEM((half, width), f32),
                pltpu.VMEM((half, width), f32),
                pltpu.VMEM((half, width), f32),
                pltpu.VMEM((BATCH, width), f32),
                dma((3, depth - 1)),
                dma((3, depth - 1)),
                dma((3, depth)),
                dma((3, depth)),
                dma((5,)),
                dma((5,)),
                dma((2,)),
                dma((nbatch,)),
                dma((nbatch,)),
                dma((nbatch,)),
                dma((nbatch,)),
                dma((nbatch,)),
                dma((1,)),
            ],
            compiler_params=pltpu.CompilerParams(
                collective_id=0, has_side_effects=True, vmem_limit_bytes=48 << 20
            ),
        )(slab, boundary, diag_inverse, sub_block, tail_coupling, tail_cols)

    placed = (
        P("row", "panel"),
        P("row", None),
        P(("panel", "row"), None),
        P(("panel", "row"), None),
        P(("panel", "row"), None),
        P(("row", "panel"), None),
    )
    return jax.shard_map(
        on_device,
        mesh=mesh,
        in_specs=placed,
        out_specs=(P("row", "panel"), P(("row", "panel"), None)),
        check_vma=False,
    )
```

```python
import functools

import jax
import jax.numpy as jnp
from jax import lax
from jax.experimental import pallas as pl
from jax.experimental.pallas import tpu as pltpu
from jax.sharding import PartitionSpec as P

MESH = pl.DeviceIdType.MESH
BATCH = 32
PIECE = 16
NT = (((1,), (1,)), ((), ()))
NN = (((1,), (0,)), ((), ()))


def split(value):
    high = value.astype(jnp.bfloat16)
    low = (value - high.astype(jnp.float32)).astype(jnp.bfloat16)
    return high, low


def dot3(left, right, dims):
    left_high, left_low = split(left)
    right_high, right_low = split(right)
    dot = functools.partial(lax.dot_general, dimension_numbers=dims, preferred_element_type=jnp.float32)
    return dot(left_high, right_high) + (dot(left_high, right_low) + dot(left_low, right_high))


def kernel(
    panels, rows,
    slab, boundary, inverse_ref, beneath_ref, coupling_ref, cols_ref,
    factor_ref, tail_ref,
    slabs, inverses, beneath, couplings, products, constants, step_high, step_low,
    offset, entering, solved, share, sums_in, sums_out, total, cols,
    z_send, z_recv, x_send, x_recv, pair_send, pair_recv, local_sem,
    y_send, y_recv, s_send, s_recv, t_send, t_recv,
):
    p, r = lax.axis_index("panel"), lax.axis_index("row")
    core = lax.rem(p, 2)
    chip = lax.div(p, 2)
    chips = panels // 2
    z, x = lax.div(r, 2), lax.rem(r, 2)
    depth = rows // 2
    half = slab.shape[0] // 2
    nbatch = half // BATCH
    width = slab.shape[1]
    mine = pl.ds(pl.multiple_of(core * half, half), half)
    other = pl.ds(pl.multiple_of((1 - core) * half, half), half)
    sibling = {"panel": p + 1 - 2 * core, "row": r}
    beside = {"panel": p, "row": r + 1 - 2 * x}
    after = {"panel": p + 2, "row": r}
    ahead = {"panel": p - 2, "row": r}
    collector = {"panel": panels - 2 + lax.div(p, panels // 2), "row": r}
    steps = sorted(range(1, depth), key=lambda d: (min(d, depth - d), d))

    def z_row(shift):
        return lax.rem(z + shift + depth, depth) * 2 + x

    local_slab = pltpu.make_async_copy(slab.at[mine], slabs.at[core], local_sem.at[0])
    local_slab.start()
    local_cols = pltpu.make_async_copy(cols_ref, cols, local_sem.at[2])
    local_cols.start()
    full = (inverses.at[core], beneath, couplings.at[core])
    shards = (inverse_ref, beneath_ref, coupling_ref)
    local_shards = [pltpu.make_async_copy(shards[k], full[k].at[r], local_sem.at[3 + k]) for k in range(3)]
    for copy in local_shards:
        copy.start()

    barrier = pltpu.get_barrier_semaphore()

    def greet(target):
        pl.semaphore_signal(barrier, inc=1, device_id=target, device_id_type=MESH)

    for shift in steps:
        greet({"panel": p, "row": z_row(shift)})
    greet(beside)
    greet(sibling)
    last = chip == chips - 1

    @pl.when(chip > 0)
    def _():
        greet(ahead)

    @pl.when(p < panels - 1)
    def _():
        greet(collector)

    gathering = jnp.where(last, panels // 2 - core, 1)
    pl.semaphore_wait(barrier, depth + 1 + gathering)

    def z_copy(k, i, shift):
        return pltpu.make_async_remote_copy(
            src_ref=shards[k], dst_ref=full[k].at[r], send_sem=z_send.at[k, i], recv_sem=z_recv.at[k, i],
            device_id={"panel": p, "row": z_row(shift)}, device_id_type=MESH,
        )

    def z_arrival(k, i, shift):
        return pltpu.make_async_remote_copy(
            src_ref=shards[k], dst_ref=full[k].at[z_row(-shift)], send_sem=z_send.at[k, i], recv_sem=z_recv.at[k, i],
            device_id={"panel": p, "row": z_row(shift)}, device_id_type=MESH,
        )

    def x_own(k):
        return pltpu.make_async_remote_copy(
            src_ref=shards[k], dst_ref=full[k].at[r], send_sem=x_send.at[k, depth - 1], recv_sem=x_recv.at[k, depth - 1],
            device_id=beside, device_id_type=MESH,
        )

    def x_relay(k, i, shift):
        place = full[k].at[z_row(-shift)]
        return pltpu.make_async_remote_copy(
            src_ref=place, dst_ref=place, send_sem=x_send.at[k, i], recv_sem=x_recv.at[k, i],
            device_id=beside, device_id_type=MESH,
        )

    def x_arrivals(k):
        x_own(k).wait_recv()
        for i, shift in enumerate(steps):
            x_relay(k, i, shift).wait_recv()

    def to_sibling(k, src, dst):
        return pltpu.make_async_remote_copy(
            src_ref=src, dst_ref=dst, send_sem=pair_send.at[k], recv_sem=pair_recv.at[k],
            device_id=sibling, device_id_type=MESH,
        )

    pair_slab = to_sibling(0, slab.at[other], slabs.at[core])
    pair_inverse = to_sibling(1, inverses.at[core], inverses.at[core])
    pair_product = to_sibling(2, products.at[core], products.at[core])
    pair_coupling = to_sibling(3, couplings.at[core], couplings.at[core])
    pair_factor = to_sibling(4, solved.at[1 - core], factor_ref.at[mine])

    for k in range(3):
        x_own(k).start()
        for i, shift in enumerate(steps):
            z_copy(k, i, shift).start()
        if k == 0:
            pair_slab.start()
    for copy in local_shards:
        copy.wait()

    def relay(k):
        for i, shift in enumerate(steps):
            z_arrival(k, i, shift).wait_recv()
            x_relay(k, i, shift).start()

    def square(ref):
        return ref[...].reshape(width, width)

    relay(0)
    relay(1)
    x_arrivals(0)
    pair_inverse.start()
    x_arrivals(1)
    products[core] = dot3(square(inverses.at[core]), square(beneath), NN)
    pair_product.start()
    local_slab.wait()
    constants[core] = dot3(slabs[core], square(inverses.at[core]), NT)
    pair_slab.wait_recv()
    pair_inverse.wait_recv()
    constants[1 - core] = dot3(slabs[1 - core], square(inverses.at[1 - core]), NT)
    pair_product.wait_recv()
    step_high[...], step_low[...] = split(dot3(products[1], products[0], NN).T)
    offset[...] = constants[1] - dot3(constants[0], products[1], NT)

    @pl.when(chip == 0)
    def _():
        load = pltpu.make_async_copy(boundary.at[mine], entering, local_sem.at[1])
        load.start()
        load.wait()

    def batch(b):
        return pl.ds(pl.multiple_of(b * BATCH, BATCH), BATCH)

    def piece(b):
        return pl.ds(pl.multiple_of(b * PIECE, PIECE), PIECE)

    def y_copy(b):
        return pltpu.make_async_remote_copy(
            src_ref=solved.at[1, piece(b)], dst_ref=entering.at[piece(b)], send_sem=y_send.at[b], recv_sem=y_recv.at[b],
            device_id=after, device_id_type=MESH,
        )

    def advance(b, carry):
        @pl.when(chip > 0)
        def _():
            y_copy(b).wait_recv()

        high, low = split(entering[piece(b)])
        both = jnp.dot(jnp.concatenate([high, low], axis=0), step_high[...], preferred_element_type=jnp.float32)
        rest = jnp.dot(high, step_low[...], preferred_element_type=jnp.float32)
        solved[1, piece(b)] = offset[piece(b)] + (both[:PIECE] + (both[PIECE:] + rest))

        @pl.when(chip < chips - 1)
        def _():
            y_copy(b).start()

        return carry

    npiece = half // PIECE
    lax.fori_loop(0, npiece // 2, advance, 0)
    relay(2)
    lax.fori_loop(npiece // 2, npiece, advance, 0)
    x_arrivals(2)
    pair_coupling.start()
    solved[0] = constants[0] - dot3(entering[...], products[0], NT)
    pair_factor.start()
    share[...] = dot3(solved[core], square(couplings.at[core]), NN)
    factor_ref[mine] = solved[core]
    pair_coupling.wait_recv()
    share[...] += dot3(solved[1 - core], square(couplings.at[1 - core]), NN)

    def s_copy(b):
        return pltpu.make_async_remote_copy(
            src_ref=sums_out.at[batch(b)], dst_ref=sums_in.at[batch(b)], send_sem=s_send.at[b], recv_sem=s_recv.at[b],
            device_id=after, device_id_type=MESH,
        )

    def t_copy(b):
        return pltpu.make_async_remote_copy(
            src_ref=sums_out.at[batch(b)], dst_ref=total, send_sem=t_send.at[b], recv_sem=t_recv.at[0],
            device_id={"panel": core * nbatch + b, "row": r}, device_id_type=MESH,
        )

    def add_up(b, carry):
        @pl.when(chip == 0)
        def _():
            sums_out[batch(b)] = share[batch(b)]

        @pl.when(chip > 0)
        def _():
            s_copy(b).wait_recv()
            sums_out[batch(b)] = sums_in[batch(b)] + share[batch(b)]

        @pl.when(chip < chips - 1)
        def _():
            s_copy(b).start()

        owner = core * nbatch + b

        @pl.when(last & (owner != p))
        def _():
            t_copy(b).start()

        @pl.when(last & (owner == p))
        def _():
            total[...] = sums_out[batch(b)]

        return carry

    lax.fori_loop(0, nbatch, add_up, 0)

    @pl.when(p < panels - 1)
    def _():
        t_copy(0).wait_recv()

    local_cols.wait()
    tail_ref[...] = cols[...] - total[...]

    def drain(b, carry):
        @pl.when(chip < chips - 1)
        def _():
            s_copy(b).wait_send()

        @pl.when(last & (core * nbatch + b != p))
        def _():
            t_copy(b).wait_send()

        return carry

    lax.fori_loop(0, nbatch, drain, 0)

    def drain_steps(b, carry):
        @pl.when(chip < chips - 1)
        def _():
            y_copy(b).wait_send()

        return carry

    lax.fori_loop(0, npiece, drain_steps, 0)
    for k in range(3):
        x_own(k).wait_send()
        for i, shift in enumerate(steps):
            z_copy(k, i, shift).wait_send()
            x_relay(k, i, shift).wait_send()
    pair_slab.wait_send()
    pair_inverse.wait_send()
    pair_product.wait_send()
    pair_coupling.wait_send()
    pair_factor.wait()


def solution(mesh):
    panels, rows = mesh.shape["panel"], mesh.shape["row"]

    def on_device(slab, boundary, diag_inverse, sub_block, tail_coupling, tail_cols):
        height, width = slab.shape
        half = height // 2
        depth = rows // 2
        nbatch = half // BATCH
        f32 = jnp.float32
        shard = diag_inverse.shape[0]
        whole = pl.BlockSpec(memory_space=pltpu.VMEM)
        apart = pl.BlockSpec(memory_space=pltpu.HBM)
        dma = pltpu.SemaphoreType.DMA
        operands = [
            pltpu.with_memory_space_constraint(value, pltpu.HBM)
            for value in (slab, boundary, diag_inverse, sub_block, tail_coupling, tail_cols)
        ]
        return pl.pallas_call(
            functools.partial(kernel, panels, rows),
            out_shape=(
                jax.ShapeDtypeStruct((height, width), f32),
                jax.ShapeDtypeStruct(tail_cols.shape, f32),
            ),
            in_specs=[apart, apart, apart, apart, apart, apart],
            out_specs=(whole, whole),
            scratch_shapes=[
                pltpu.VMEM((2, half, width), f32),
                pltpu.VMEM((2, rows, shard, width), f32),
                pltpu.VMEM((rows, shard, width), f32),
                pltpu.VMEM((2, rows, shard, width), f32),
                pltpu.VMEM((2, width, width), f32),
                pltpu.VMEM((2, half, width), f32),
                pltpu.VMEM((width, width), jnp.bfloat16),
                pltpu.VMEM((width, width), jnp.bfloat16),
                pltpu.VMEM((half, width), f32),
                pltpu.VMEM((half, width), f32),
                pltpu.VMEM((2, half, width), f32),
                pltpu.VMEM((half, width), f32),
                pltpu.VMEM((half, width), f32),
                pltpu.VMEM((half, width), f32),
                pltpu.VMEM((BATCH, width), f32),
                pltpu.VMEM(tail_cols.shape, f32),
                dma((3, depth - 1)),
                dma((3, depth - 1)),
                dma((3, depth)),
                dma((3, depth)),
                dma((5,)),
                dma((5,)),
                dma((6,)),
                dma((half // PIECE,)),
                dma((half // PIECE,)),
                dma((nbatch,)),
                dma((nbatch,)),
                dma((nbatch,)),
                dma((1,)),
            ],
            compiler_params=pltpu.CompilerParams(
                collective_id=0, has_side_effects=True, vmem_limit_bytes=48 << 20
            ),
        )(*operands)

    placed = (
        P("row", "panel"),
        P("row", None),
        P(("panel", "row"), None),
        P(("panel", "row"), None),
        P(("panel", "row"), None),
        P(("row", "panel"), None),
    )
    return jax.shard_map(
        on_device,
        mesh=mesh,
        in_specs=placed,
        out_specs=(P("row", "panel"), P(("row", "panel"), None)),
        check_vma=False,
    )
```

```python
import functools

import jax
import jax.numpy as jnp
from jax import lax
from jax.experimental import pallas as pl
from jax.experimental.pallas import tpu as pltpu
from jax.sharding import PartitionSpec as P

MESH = pl.DeviceIdType.MESH
STEP = 32
GROUP = 4
NT = (((1,), (1,)), ((), ()))
NN = (((1,), (0,)), ((), ()))


def split(value):
    high = value.astype(jnp.bfloat16)
    low = (value - high.astype(jnp.float32)).astype(jnp.bfloat16)
    return high, low


def dot3(left, right, dims):
    left_high, left_low = split(left)
    right_high, right_low = split(right)
    dot = functools.partial(lax.dot_general, dimension_numbers=dims, preferred_element_type=jnp.float32)
    return dot(left_high, right_high) + (dot(left_high, right_low) + dot(left_low, right_high))


def kernel(
    panels, rows,
    slab, boundary, inverse_ref, beneath_ref, coupling_ref, cols_ref,
    factor_ref, tail_ref,
    slabs, inverses, beneath, couplings, products, constants, offset, entering, solved,
    sums_in, sums_out, inflow, passed, carry, carry_even, carry_sum, weight_high, weight_low, share, total, cols,
    z_send, z_recv, x_send, x_recv, g_send, g_recv, pair_send, pair_recv, local_sem,
    y_send, y_recv, t_send, t_recv, in_send, in_recv, lead_send, relay_send, u_send, u_recv,
):
    p, r = lax.axis_index("panel"), lax.axis_index("row")
    core = lax.rem(p, 2)
    chip = lax.div(p, 2)
    chips = panels // 2
    groups = chips // GROUP
    group, spot = lax.div(chip, GROUP), lax.rem(chip, GROUP)
    side = lax.div(p, panels // 2)
    z, x = lax.div(r, 2), lax.rem(r, 2)
    depth = rows // 2
    half = slab.shape[0] // 2
    width = slab.shape[1]
    head = width // 2
    n_head, n_data = head // STEP, half // STEP
    n_all = n_head + n_data
    body = pl.ds(head, half)
    mine = pl.ds(pl.multiple_of(core * half, half), half)
    other = pl.ds(pl.multiple_of((1 - core) * half, half), half)
    steps = sorted(range(1, depth), key=lambda d: (min(d, depth - d), d))

    first, final = spot == 0, spot == GROUP - 1
    carried = group > 0
    feeds = final & (group < groups - 1)

    def at(panel):
        return {"panel": panel, "row": r}

    sibling = at(p + 1 - 2 * core)
    beside = {"panel": p, "row": r + 1 - 2 * x}
    after, ahead = at(p + 2), at(p - 2)
    skip_after, skip_ahead = at(p + 2 * GROUP), at(p - 2 * GROUP)
    source_panels = [2 * (GROUP * k + GROUP - 1) for k in range(groups)]

    def z_row(shift):
        return lax.rem(z + shift + depth, depth) * 2 + x

    def any_row(shift):
        return lax.rem(r + shift + rows, rows)

    local_slab = pltpu.make_async_copy(slab.at[mine], slabs.at[core], local_sem.at[0])
    local_slab.start()
    local_cols = pltpu.make_async_copy(cols_ref, cols, local_sem.at[1])
    local_cols.start()
    local_boundary = pltpu.make_async_copy(boundary.at[mine], entering.at[body], local_sem.at[2])

    @pl.when(chip == 0)
    def _():
        local_boundary.start()

    full = (inverses.at[core], beneath, couplings.at[core])
    shards = (inverse_ref, beneath_ref, coupling_ref)
    local_shards = [pltpu.make_async_copy(shards[k], full[k].at[r], local_sem.at[3 + k]) for k in range(3)]
    for copy in local_shards:
        copy.start()

    barrier = pltpu.get_barrier_semaphore()

    def greet(target):
        pl.semaphore_signal(barrier, inc=1, device_id=target, device_id_type=MESH)

    for shift in range(1, rows):
        greet({"panel": p, "row": any_row(shift)})
    greet(sibling)

    @pl.when(chip > 0)
    def _():
        greet(ahead)

    @pl.when(carried & (spot == GROUP - 2))
    def _():
        greet(after)

    @pl.when(final & carried)
    def _():
        greet(skip_ahead)

    for start in source_panels:
        @pl.when(start + side != p)
        def _():
            greet(at(start + side))

    expected = (
        rows + jnp.where(chip < chips - 1, 1, 0) + jnp.where(carried & final, 1, 0) + jnp.where(feeds, 1, 0)
        + jnp.where(final, jnp.where(side == core, n_data - 1, n_data), 0)
    )
    pl.semaphore_wait(barrier, expected)

    def remote(src, dst, send, recv, target):
        return pltpu.make_async_remote_copy(
            src_ref=src, dst_ref=dst, send_sem=send, recv_sem=recv, device_id=target, device_id_type=MESH
        )

    def z_copy(k, i, shift, place):
        return remote(
            shards[k], full[k].at[place], z_send.at[k, i], z_recv.at[k, i], {"panel": p, "row": z_row(shift)}
        )

    def x_own(k):
        return remote(shards[k], full[k].at[r], x_send.at[k, depth - 1], x_recv.at[k, depth - 1], beside)

    def x_relay(k, i, shift):
        place = full[k].at[z_row(-shift)]
        return remote(place, place, x_send.at[k, i], x_recv.at[k, i], beside)

    def g_copy(shift, place):
        return remote(
            shards[2], full[2].at[place], g_send.at[shift - 1], g_recv.at[shift - 1],
            {"panel": p, "row": any_row(shift)},
        )

    def to_sibling(k, src, dst):
        return remote(src, dst, pair_send.at[k], pair_recv.at[k], sibling)

    pair_slab = to_sibling(0, slab.at[other], slabs.at[core])
    pair_inverse = to_sibling(1, inverses.at[core], inverses.at[core])
    pair_product = to_sibling(2, products.at[core], products.at[core])
    pair_coupling = to_sibling(3, couplings.at[core], couplings.at[core])
    pair_carry = to_sibling(4, solved.at[1, pl.ds(0, head)], carry.at[core])
    pair_even = to_sibling(5, solved.at[0, pl.ds(0, head)], carry_even.at[core])
    pair_sum = to_sibling(6, sums_out.at[pl.ds(0, head)], carry_sum.at[core])
    pair_factor = to_sibling(7, solved.at[1 - core, body], factor_ref.at[mine])

    for k in range(2):
        x_own(k).start()
        for i, shift in enumerate(steps):
            z_copy(k, i, shift, r).start()
        if k == 0:
            pair_slab.start()
    for shift in range(1, rows):
        g_copy(shift, r).start()
    for copy in local_shards:
        copy.wait()

    def relay(k):
        for i, shift in enumerate(steps):
            z_copy(k, i, shift, z_row(-shift)).wait_recv()
            x_relay(k, i, shift).start()

    def x_arrivals(k):
        x_own(k).wait_recv()
        for i, shift in enumerate(steps):
            x_relay(k, i, shift).wait_recv()

    def square(ref):
        return ref[...].reshape(width, width)

    def keep(k, value):
        weight_high[k], weight_low[k] = split(value)

    def times(value, k):
        high, low = split(value)
        count = value.shape[0]
        both = jnp.dot(jnp.concatenate([high, low], axis=0), weight_high[k], preferred_element_type=jnp.float32)
        rest = jnp.dot(high, weight_low[k], preferred_element_type=jnp.float32)
        return both[:count] + (both[count:] + rest)

    zeros = jnp.zeros((head, width), jnp.float32)
    offset[:head] = zeros
    constants[0, :head] = zeros

    @pl.when(first)
    def _():
        row = lax.broadcasted_iota(jnp.int32, (head, width), 0) + core * head
        column = lax.broadcasted_iota(jnp.int32, (head, width), 1)
        entering[:head] = jnp.where(row == column, 1.0, 0.0)

    @pl.when(first & carried)
    def _():
        entering[body] = jnp.zeros((half, width), jnp.float32)

    relay(0)
    relay(1)
    x_arrivals(0)
    pair_inverse.start()
    x_arrivals(1)
    products[core] = dot3(square(inverses.at[core]), square(beneath), NN)
    pair_product.start()
    local_slab.wait()
    constants[core, body] = dot3(slabs[core], square(inverses.at[core]), NT)
    pair_slab.wait_recv()
    pair_inverse.wait_recv()
    constants[1 - core, body] = dot3(slabs[1 - core], square(inverses.at[1 - core]), NT)
    pair_product.wait_recv()
    keep(0, dot3(products[1], products[0], NN).T)
    offset[body] = constants[1, body] - dot3(constants[0, body], products[1], NT)
    keep(1, products[0].T)

    @pl.when(chip == 0)
    def _():
        local_boundary.wait()

    def batch(b):
        return pl.ds(pl.multiple_of(b * STEP, STEP), STEP)

    def data(b):
        return pl.ds(pl.multiple_of(b * STEP + head, STEP), STEP)

    def y_copy(b):
        return remote(solved.at[1, batch(b)], entering.at[batch(b)], y_send.at[b], y_recv.at[b], after)

    def t_copy(b):
        return remote(sums_out.at[batch(b)], sums_in.at[batch(b)], t_send.at[b], t_recv.at[b], after)

    def in_copy(b):
        return remote(passed.at[batch(b)], inflow.at[batch(b)], in_send.at[b], in_recv.at[b], skip_after)

    def lead_copy(b):
        return remote(passed.at[batch(b)], inflow.at[batch(b)], lead_send.at[b], in_recv.at[b], after)

    def back_copy(b):
        return remote(inflow.at[batch(b)], inflow.at[batch(b)], relay_send.at[b], in_recv.at[b], ahead)

    def forth_copy(b):
        return remote(inflow.at[batch(b)], inflow.at[batch(b)], relay_send.at[b], in_recv.at[b], after)

    def u_copy(b):
        return remote(
            share.at[batch(b)], total.at[group], u_send.at[b], u_recv.at[group], at(core * n_data + b)
        )

    begin = jnp.where(carried, 0, n_head)
    couple_turn = n_all - 4
    inflow_lag = jnp.where(final, 7 * group, 2 * n_all)
    sum_lag = jnp.where(feeds & carried, inflow_lag + n_data, n_all)
    share_lag = sum_lag + n_head + 4
    turns = 2 * n_all + n_data

    def turn(i, unused):
        @pl.when((i >= begin) & (i < n_all))
        def _():
            @pl.when(spot > 0)
            def _():
                y_copy(i).wait_recv()

            row = offset[batch(i)] + times(entering[batch(i)], 0)
            solved[1, batch(i)] = row

            @pl.when(spot < GROUP - 1)
            def _():
                y_copy(i).start()

            @pl.when(final & (group == 0))
            def _():
                passed[batch(i - n_head)] = row
                in_copy(i - n_head).start()
                lead_copy(i - n_head).start()

        @pl.when(carried & (i == n_head))
        def _():
            pair_carry.start()
            carry[core] = solved[1, :head]

        @pl.when(i == couple_turn)
        def _():
            for shift in range(1, rows):
                g_copy(shift, any_row(-shift)).wait_recv()
            pair_coupling.start()

        @pl.when(i == sum_lag)
        def _():
            pair_coupling.wait_recv()
            keep(2, square(couplings.at[0]))
            keep(3, square(couplings.at[1]))

        b = i - sum_lag

        @pl.when((b >= begin) & (b < n_all))
        def _():
            even = constants[0, batch(b)] - times(entering[batch(b)], 1)
            solved[0, batch(b)] = even
            part = times(even, 2) + times(solved[1, batch(b)], 3)

            @pl.when(first)
            def _():
                sums_out[batch(b)] = part

            @pl.when(spot > 0)
            def _():
                t_copy(b).wait_recv()
                sums_out[batch(b)] = sums_in[batch(b)] + part

            @pl.when(spot < GROUP - 1)
            def _():
                t_copy(b).start()

        @pl.when(carried & (b == n_head))
        def _():
            pair_even.start()
            carry_even[core] = solved[0, :head]

        @pl.when(carried & final & (b == n_head))
        def _():
            pair_sum.start()
            carry_sum[core] = sums_out[:head]

        @pl.when(carried & final & (i == inflow_lag))
        def _():
            pair_carry.wait_recv()
            keep(4, carry[...].reshape(width, width))

        m = i - inflow_lag

        @pl.when(carried & (first | final) & (m >= 0) & (m < n_data))
        def _():
            in_copy(m).wait_recv()

            @pl.when(first)
            def _():
                forth_copy(m).start()

            @pl.when(final & jnp.logical_not(feeds))
            def _():
                back_copy(m).start()

            @pl.when(final)
            def _():
                passed[batch(m)] = solved[1, data(m)] + times(inflow[batch(m)], 4)

            @pl.when(feeds)
            def _():
                in_copy(m).start()
                lead_copy(m).start()

        @pl.when(carried & feeds & (m == n_data))
        def _():
            def hand_back(k, unused):
                back_copy(k).start()
                return unused

            lax.fori_loop(0, n_data, hand_back, 0)

        @pl.when(carried & final & (i == share_lag))
        def _():
            pair_sum.wait_recv()
            keep(6, carry_sum[...].reshape(width, width))

        t = i - share_lag

        @pl.when(final & (t >= 0) & (t < n_data))
        def _():
            @pl.when(carried)
            def _():
                share[batch(t)] = sums_out[data(t)] + times(inflow[batch(t)], 6)

            @pl.when(group == 0)
            def _():
                share[batch(t)] = sums_out[data(t)]

            @pl.when(core * n_data + t != p)
            def _():
                u_copy(t).start()

            @pl.when(core * n_data + t == p)
            def _():
                total[group] = share[batch(t)]

        return unused

    lax.fori_loop(0, turns, turn, 0)

    @pl.when(final & carried)
    def _():
        solved[1, body] = passed[...]

    @pl.when(spot < GROUP - 1)
    def _():
        def sent(b, unused):
            y_copy(b).wait_send()
            t_copy(b).wait_send()
            return unused

        lax.fori_loop(begin, n_all, sent, 0)

    @pl.when(carried & (spot > 0) & (spot < GROUP - 1))
    def _():
        def reached(b, unused):
            in_copy(b).wait_recv()
            return unused

        lax.fori_loop(0, n_data, reached, 0)

    @pl.when(carried & (spot < GROUP - 1))
    def _():
        pair_carry.wait_recv()
        keep(4, carry[...].reshape(width, width))
        solved[1, body] += times(inflow[...], 4)

    @pl.when(carried)
    def _():
        pair_even.wait_recv()
        keep(5, carry_even[...].reshape(width, width))
        solved[0, body] += times(inflow[...], 5)

    pair_factor.start()
    factor_ref[mine] = solved[core, body]

    for k, start in enumerate(source_panels):
        @pl.when(start + side != p)
        def _():
            remote(share.at[batch(0)], total.at[k], u_send.at[0], u_recv.at[k], at(start + side)).wait_recv()

    local_cols.wait()
    summed = total[0]
    for k in range(1, groups):
        summed = summed + total[k]
    tail_ref[...] = cols[...] - summed

    def drain(b, unused):
        @pl.when(feeds)
        def _():
            in_copy(b).wait_send()
            lead_copy(b).wait_send()

        @pl.when(carried & (first | final))
        def _():
            back_copy(b).wait_send()

        @pl.when(final & (core * n_data + b != p))
        def _():
            u_copy(b).wait_send()

        return unused

    lax.fori_loop(0, n_data, drain, 0)

    for k in range(2):
        x_own(k).wait_send()
        for i, shift in enumerate(steps):
            z_copy(k, i, shift, r).wait_send()
            x_relay(k, i, shift).wait_send()
    for shift in range(1, rows):
        g_copy(shift, r).wait_send()
    pair_slab.wait_send()
    pair_inverse.wait_send()
    pair_product.wait_send()
    pair_coupling.wait_send()

    @pl.when(carried)
    def _():
        pair_carry.wait_send()
        pair_even.wait_send()

    @pl.when(carried & final)
    def _():
        pair_sum.wait_send()

    pair_factor.wait()


def solution(mesh):
    panels, rows = mesh.shape["panel"], mesh.shape["row"]

    def on_device(slab, boundary, diag_inverse, sub_block, tail_coupling, tail_cols):
        height, width = slab.shape
        half, head = height // 2, width // 2
        extended = head + half
        depth = rows // 2
        n_data, n_all = half // STEP, extended // STEP
        groups = panels // 2 // GROUP
        f32, bf16 = jnp.float32, jnp.bfloat16
        shard = diag_inverse.shape[0]
        whole = pl.BlockSpec(memory_space=pltpu.VMEM)
        apart = pl.BlockSpec(memory_space=pltpu.HBM)
        dma = pltpu.SemaphoreType.DMA
        operands = [
            pltpu.with_memory_space_constraint(value, pltpu.HBM)
            for value in (slab, boundary, diag_inverse, sub_block, tail_coupling, tail_cols)
        ]
        return pl.pallas_call(
            functools.partial(kernel, panels, rows),
            out_shape=(
                jax.ShapeDtypeStruct((height, width), f32),
                jax.ShapeDtypeStruct(tail_cols.shape, f32),
            ),
            in_specs=[apart] * 6,
            out_specs=(whole, whole),
            scratch_shapes=[
                pltpu.VMEM((2, half, width), f32),
                pltpu.VMEM((2, rows, shard, width), f32),
                pltpu.VMEM((rows, shard, width), f32),
                pltpu.VMEM((2, rows, shard, width), f32),
                pltpu.VMEM((2, width, width), f32),
                pltpu.VMEM((2, extended, width), f32),
                pltpu.VMEM((extended, width), f32),
                pltpu.VMEM((extended, width), f32),
                pltpu.VMEM((2, extended, width), f32),
                pltpu.VMEM((extended, width), f32),
                pltpu.VMEM((extended, width), f32),
                pltpu.VMEM((half, width), f32),
                pltpu.VMEM((half, width), f32),
                pltpu.VMEM((2, head, width), f32),
                pltpu.VMEM((2, head, width), f32),
                pltpu.VMEM((2, head, width), f32),
                pltpu.VMEM((7, width, width), bf16),
                pltpu.VMEM((7, width, width), bf16),
                pltpu.VMEM((half, width), f32),
                pltpu.VMEM((groups, STEP, width), f32),
                pltpu.VMEM(tail_cols.shape, f32),
                dma((2, depth - 1)),
                dma((2, depth - 1)),
                dma((2, depth)),
                dma((2, depth)),
                dma((rows - 1,)),
                dma((rows - 1,)),
                dma((8,)),
                dma((8,)),
                dma((6,)),
                dma((n_all,)),
                dma((n_all,)),
                dma((n_all,)),
                dma((n_all,)),
                dma((n_data,)),
                dma((n_data,)),
                dma((n_data,)),
                dma((n_data,)),
                dma((n_data,)),
                dma((groups,)),
            ],
            compiler_params=pltpu.CompilerParams(
                collective_id=0, has_side_effects=True, vmem_limit_bytes=48 << 20
            ),
        )(*operands)

    placed = (
        P("row", "panel"),
        P("row", None),
        P(("panel", "row"), None),
        P(("panel", "row"), None),
        P(("panel", "row"), None),
        P(("row", "panel"), None),
    )
    return jax.shard_map(
        on_device,
        mesh=mesh,
        in_specs=placed,
        out_specs=(P("row", "panel"), P(("row", "panel"), None)),
        check_vma=False,
    )
```

```python
import functools

import jax
import jax.numpy as jnp
from jax import lax
from jax.experimental import pallas as pl
from jax.experimental.pallas import tpu as pltpu
from jax.sharding import PartitionSpec as P

MESH = pl.DeviceIdType.MESH
STEP = 32
GROUP = 4
NT = (((1,), (1,)), ((), ()))
NN = (((1,), (0,)), ((), ()))


def split(value):
    high = value.astype(jnp.bfloat16)
    low = (value - high.astype(jnp.float32)).astype(jnp.bfloat16)
    return high, low


def dot3(left, right, dims):
    left_high, left_low = split(left)
    right_high, right_low = split(right)
    dot = functools.partial(lax.dot_general, dimension_numbers=dims, preferred_element_type=jnp.float32)
    return dot(left_high, right_high) + (dot(left_high, right_low) + dot(left_low, right_high))


def kernel(
    panels, rows,
    slab, boundary, inverse_ref, beneath_ref, coupling_ref, cols_ref,
    factor_ref, tail_ref,
    slabs, inverses, beneath, couplings, products, constants, offset, entering, solved,
    sums_in, sums_out, inflow, passed, carry, carry_even, carry_sum, weight_high, weight_low, share, total, cols,
    z_send, z_recv, x_send, x_recv, g_send, g_recv, pair_send, pair_recv, local_sem,
    y_send, y_recv, t_send, t_recv, in_send, in_recv, lead_send, relay_send, u_send, u_recv,
):
    p, r = lax.axis_index("panel"), lax.axis_index("row")
    core = lax.rem(p, 2)
    chip = lax.div(p, 2)
    chips = panels // 2
    groups = chips // GROUP
    group, spot = lax.div(chip, GROUP), lax.rem(chip, GROUP)
    side = lax.div(p, panels // 2)
    z, x = lax.div(r, 2), lax.rem(r, 2)
    depth = rows // 2
    half = slab.shape[0] // 2
    width = slab.shape[1]
    head = width // 2
    n_head, n_data = head // STEP, half // STEP
    n_all = n_head + n_data
    body = pl.ds(head, half)
    mine = pl.ds(pl.multiple_of(core * half, half), half)
    other = pl.ds(pl.multiple_of((1 - core) * half, half), half)
    steps = sorted(range(1, depth), key=lambda d: (min(d, depth - d), d))

    first, final = spot == 0, spot == GROUP - 1
    carried = group > 0
    feeds = final & (group < groups - 1)

    def at(panel):
        return {"panel": panel, "row": r}

    sibling = at(p + 1 - 2 * core)
    beside = {"panel": p, "row": r + 1 - 2 * x}
    after, ahead = at(p + 2), at(p - 2)
    skip_after, skip_ahead = at(p + 2 * GROUP), at(p - 2 * GROUP)
    source_panels = [2 * (GROUP * k + GROUP - 1) for k in range(groups)]

    def z_row(shift):
        return lax.rem(z + shift + depth, depth) * 2 + x

    def any_row(shift):
        return lax.rem(r + shift + rows, rows)

    local_slab = pltpu.make_async_copy(slab.at[mine], slabs.at[core], local_sem.at[0])
    local_slab.start()
    local_cols = pltpu.make_async_copy(cols_ref, cols, local_sem.at[1])
    local_cols.start()
    local_boundary = pltpu.make_async_copy(boundary.at[mine], entering.at[body], local_sem.at[2])

    @pl.when(chip == 0)
    def _():
        local_boundary.start()

    full = (inverses.at[core], beneath, couplings.at[core])
    shards = (inverse_ref, beneath_ref, coupling_ref)
    local_shards = [pltpu.make_async_copy(shards[k], full[k].at[r], local_sem.at[3 + k]) for k in range(3)]
    for copy in local_shards:
        copy.start()

    barrier = pltpu.get_barrier_semaphore()

    def greet(target):
        pl.semaphore_signal(barrier, inc=1, device_id=target, device_id_type=MESH)

    for shift in range(1, rows):
        greet({"panel": p, "row": any_row(shift)})
    greet(sibling)

    @pl.when(chip > 0)
    def _():
        greet(ahead)

    @pl.when(final & carried)
    def _():
        greet(skip_ahead)

    for start in source_panels:
        @pl.when(start + side != p)
        def _():
            greet(at(start + side))

    expected = (
        rows + jnp.where(chip < chips - 1, 1, 0) + jnp.where(feeds, 1, 0)
        + jnp.where(final, jnp.where(side == core, n_data - 1, n_data), 0)
    )
    pl.semaphore_wait(barrier, expected)

    def remote(src, dst, send, recv, target):
        return pltpu.make_async_remote_copy(
            src_ref=src, dst_ref=dst, send_sem=send, recv_sem=recv, device_id=target, device_id_type=MESH
        )

    def z_copy(k, i, shift, place):
        return remote(
            shards[k], full[k].at[place], z_send.at[k, i], z_recv.at[k, i], {"panel": p, "row": z_row(shift)}
        )

    def x_own(k):
        return remote(shards[k], full[k].at[r], x_send.at[k, depth - 1], x_recv.at[k, depth - 1], beside)

    def x_relay(k, i, shift):
        place = full[k].at[z_row(-shift)]
        return remote(place, place, x_send.at[k, i], x_recv.at[k, i], beside)

    def g_copy(shift, place):
        return remote(
            shards[2], full[2].at[place], g_send.at[shift - 1], g_recv.at[shift - 1],
            {"panel": p, "row": any_row(shift)},
        )

    def to_sibling(k, src, dst):
        return remote(src, dst, pair_send.at[k], pair_recv.at[k], sibling)

    pair_slab = to_sibling(0, slab.at[other], slabs.at[core])
    pair_inverse = to_sibling(1, inverses.at[core], inverses.at[core])
    pair_product = to_sibling(2, products.at[core], products.at[core])
    pair_coupling = to_sibling(3, couplings.at[core], couplings.at[core])
    pair_carry = to_sibling(4, solved.at[1, pl.ds(0, head)], carry.at[core])
    pair_even = to_sibling(5, solved.at[0, pl.ds(0, head)], carry_even.at[core])
    pair_sum = to_sibling(6, sums_out.at[pl.ds(0, head)], carry_sum.at[core])
    pair_factor = to_sibling(7, solved.at[1 - core, body], factor_ref.at[mine])

    for k in range(2):
        x_own(k).start()
        for i, shift in enumerate(steps):
            z_copy(k, i, shift, r).start()
        if k == 0:
            pair_slab.start()
    for copy in local_shards:
        copy.wait()

    def relay(k):
        for i, shift in enumerate(steps):
            z_copy(k, i, shift, z_row(-shift)).wait_recv()
            x_relay(k, i, shift).start()

    def x_arrivals(k):
        x_own(k).wait_recv()
        for i, shift in enumerate(steps):
            x_relay(k, i, shift).wait_recv()

    def square(ref):
        return ref[...].reshape(width, width)

    def keep(k, value):
        weight_high[k], weight_low[k] = split(value)

    def times(value, k):
        high, low = split(value)
        count = value.shape[0]
        both = jnp.dot(jnp.concatenate([high, low], axis=0), weight_high[k], preferred_element_type=jnp.float32)
        rest = jnp.dot(high, weight_low[k], preferred_element_type=jnp.float32)
        return both[:count] + (both[count:] + rest)

    zeros = jnp.zeros((head, width), jnp.float32)
    offset[:head] = zeros
    constants[0, :head] = zeros

    @pl.when(first)
    def _():
        row = lax.broadcasted_iota(jnp.int32, (head, width), 0) + core * head
        column = lax.broadcasted_iota(jnp.int32, (head, width), 1)
        entering[:head] = jnp.where(row == column, 1.0, 0.0)

    @pl.when(first & carried)
    def _():
        entering[body] = jnp.zeros((half, width), jnp.float32)

    relay(0)
    relay(1)
    for shift in range(1, rows):
        g_copy(shift, r).start()
    x_arrivals(0)
    pair_inverse.start()
    x_arrivals(1)
    products[core] = dot3(square(inverses.at[core]), square(beneath), NN)
    pair_product.start()
    local_slab.wait()
    constants[core, body] = dot3(slabs[core], square(inverses.at[core]), NT)
    pair_slab.wait_recv()
    pair_inverse.wait_recv()
    constants[1 - core, body] = dot3(slabs[1 - core], square(inverses.at[1 - core]), NT)
    pair_product.wait_recv()
    keep(0, dot3(products[1], products[0], NN).T)
    offset[body] = constants[1, body] - dot3(constants[0, body], products[1], NT)
    keep(1, products[0].T)

    @pl.when(chip == 0)
    def _():
        local_boundary.wait()

    def batch(b):
        return pl.ds(pl.multiple_of(b * STEP, STEP), STEP)

    def data(b):
        return pl.ds(pl.multiple_of(b * STEP + head, STEP), STEP)

    def y_copy(b):
        return remote(solved.at[1, batch(b)], entering.at[batch(b)], y_send.at[b], y_recv.at[b], after)

    def t_copy(b):
        return remote(sums_out.at[batch(b)], sums_in.at[batch(b)], t_send.at[b], t_recv.at[b], after)

    def in_copy(b):
        return remote(passed.at[batch(b)], inflow.at[batch(b)], in_send.at[b], in_recv.at[b], skip_after)

    def lead_copy(b):
        return remote(passed.at[batch(b)], inflow.at[batch(b)], lead_send.at[b], in_recv.at[b], after)

    def relay_copy(b):
        return remote(inflow.at[batch(b)], inflow.at[batch(b)], relay_send.at[b], in_recv.at[b], after)

    def u_copy(b):
        return remote(
            share.at[batch(b)], total.at[group], u_send.at[b], u_recv.at[group], at(core * n_data + b)
        )

    begin = jnp.where(carried, 0, n_head)
    couple_turn = n_all - 4
    relays = carried & (spot < GROUP - 2)
    inflow_lag = jnp.where(final, 4 + 8 * group, 2 * n_all)
    sum_lag = n_all
    share_lag = jnp.maximum(sum_lag + 8, inflow_lag + 1)
    turns = 2 * n_all + n_data

    def turn(i, unused):
        @pl.when((i >= begin) & (i < n_all))
        def _():
            @pl.when(spot > 0)
            def _():
                y_copy(i).wait_recv()

            row = offset[batch(i)] + times(entering[batch(i)], 0)
            solved[1, batch(i)] = row

            @pl.when(spot < GROUP - 1)
            def _():
                y_copy(i).start()

            @pl.when(final & (group == 0))
            def _():
                passed[batch(i - n_head)] = row
                in_copy(i - n_head).start()
                lead_copy(i - n_head).start()

        @pl.when(carried & (i == n_head))
        def _():
            pair_carry.start()
            carry[core] = solved[1, :head]

        @pl.when(i == couple_turn)
        def _():
            for shift in range(1, rows):
                g_copy(shift, any_row(-shift)).wait_recv()
            pair_coupling.start()

        @pl.when(i == sum_lag)
        def _():
            pair_coupling.wait_recv()
            keep(2, square(couplings.at[0]))
            keep(3, square(couplings.at[1]))

        b = i - sum_lag

        @pl.when((b >= begin) & (b < n_all))
        def _():
            even = constants[0, batch(b)] - times(entering[batch(b)], 1)
            solved[0, batch(b)] = even
            part = times(even, 2) + times(solved[1, batch(b)], 3)

            @pl.when(first)
            def _():
                sums_out[batch(b)] = part

            @pl.when(spot > 0)
            def _():
                t_copy(b).wait_recv()
                sums_out[batch(b)] = sums_in[batch(b)] + part

            @pl.when(spot < GROUP - 1)
            def _():
                t_copy(b).start()

        @pl.when(carried & (b == n_head))
        def _():
            pair_even.start()
            carry_even[core] = solved[0, :head]

        @pl.when(carried & final & (b == n_head))
        def _():
            pair_sum.start()
            carry_sum[core] = sums_out[:head]

        @pl.when(carried & final & (i == inflow_lag))
        def _():
            pair_carry.wait_recv()
            keep(4, carry[...].reshape(width, width))

        m = i - inflow_lag

        @pl.when((relays | (carried & final)) & (m >= 0) & (m < n_data))
        def _():
            in_copy(m).wait_recv()

            @pl.when(relays)
            def _():
                relay_copy(m).start()

            @pl.when(final)
            def _():
                passed[batch(m)] = solved[1, data(m)] + times(inflow[batch(m)], 4)

            @pl.when(feeds)
            def _():
                in_copy(m).start()
                lead_copy(m).start()

        @pl.when(carried & final & (i == share_lag))
        def _():
            pair_sum.wait_recv()
            keep(6, carry_sum[...].reshape(width, width))

        t = i - share_lag

        @pl.when(final & (t >= 0) & (t < n_data))
        def _():
            @pl.when(carried)
            def _():
                share[batch(t)] = sums_out[data(t)] + times(inflow[batch(t)], 6)

            @pl.when(group == 0)
            def _():
                share[batch(t)] = sums_out[data(t)]

            @pl.when(core * n_data + t != p)
            def _():
                u_copy(t).start()

            @pl.when(core * n_data + t == p)
            def _():
                total[group] = share[batch(t)]

        return unused

    lax.fori_loop(0, turns, turn, 0)

    @pl.when(final & carried)
    def _():
        solved[1, body] = passed[...]

    @pl.when(spot < GROUP - 1)
    def _():
        def sent(b, unused):
            y_copy(b).wait_send()
            t_copy(b).wait_send()
            return unused

        lax.fori_loop(begin, n_all, sent, 0)

    @pl.when(carried & (spot == GROUP - 2))
    def _():
        def reached(b, unused):
            in_copy(b).wait_recv()
            return unused

        lax.fori_loop(0, n_data, reached, 0)

    @pl.when(carried & (spot < GROUP - 1))
    def _():
        pair_carry.wait_recv()
        keep(4, carry[...].reshape(width, width))
        solved[1, body] += times(inflow[...], 4)

    @pl.when(carried)
    def _():
        pair_even.wait_recv()
        keep(5, carry_even[...].reshape(width, width))
        solved[0, body] += times(inflow[...], 5)

    pair_factor.start()
    factor_ref[mine] = solved[core, body]

    for k, start in enumerate(source_panels):
        @pl.when(start + side != p)
        def _():
            remote(share.at[batch(0)], total.at[k], u_send.at[0], u_recv.at[k], at(start + side)).wait_recv()

    local_cols.wait()
    summed = total[0]
    for k in range(1, groups):
        summed = summed + total[k]
    tail_ref[...] = cols[...] - summed

    def drain(b, unused):
        @pl.when(feeds)
        def _():
            in_copy(b).wait_send()
            lead_copy(b).wait_send()

        @pl.when(relays)
        def _():
            relay_copy(b).wait_send()

        @pl.when(final & (core * n_data + b != p))
        def _():
            u_copy(b).wait_send()

        return unused

    lax.fori_loop(0, n_data, drain, 0)

    for k in range(2):
        x_own(k).wait_send()
        for i, shift in enumerate(steps):
            z_copy(k, i, shift, r).wait_send()
            x_relay(k, i, shift).wait_send()
    for shift in range(1, rows):
        g_copy(shift, r).wait_send()
    pair_slab.wait_send()
    pair_inverse.wait_send()
    pair_product.wait_send()
    pair_coupling.wait_send()

    @pl.when(carried)
    def _():
        pair_carry.wait_send()
        pair_even.wait_send()

    @pl.when(carried & final)
    def _():
        pair_sum.wait_send()

    pair_factor.wait()


def solution(mesh):
    panels, rows = mesh.shape["panel"], mesh.shape["row"]

    def on_device(slab, boundary, diag_inverse, sub_block, tail_coupling, tail_cols):
        height, width = slab.shape
        half, head = height // 2, width // 2
        extended = head + half
        depth = rows // 2
        n_data, n_all = half // STEP, extended // STEP
        groups = panels // 2 // GROUP
        f32, bf16 = jnp.float32, jnp.bfloat16
        shard = diag_inverse.shape[0]
        whole = pl.BlockSpec(memory_space=pltpu.VMEM)
        apart = pl.BlockSpec(memory_space=pltpu.HBM)
        dma = pltpu.SemaphoreType.DMA
        operands = [
            pltpu.with_memory_space_constraint(value, pltpu.HBM)
            for value in (slab, boundary, diag_inverse, sub_block, tail_coupling, tail_cols)
        ]
        return pl.pallas_call(
            functools.partial(kernel, panels, rows),
            out_shape=(
                jax.ShapeDtypeStruct((height, width), f32),
                jax.ShapeDtypeStruct(tail_cols.shape, f32),
            ),
            in_specs=[apart] * 6,
            out_specs=(whole, whole),
            scratch_shapes=[
                pltpu.VMEM((2, half, width), f32),
                pltpu.VMEM((2, rows, shard, width), f32),
                pltpu.VMEM((rows, shard, width), f32),
                pltpu.VMEM((2, rows, shard, width), f32),
                pltpu.VMEM((2, width, width), f32),
                pltpu.VMEM((2, extended, width), f32),
                pltpu.VMEM((extended, width), f32),
                pltpu.VMEM((extended, width), f32),
                pltpu.VMEM((2, extended, width), f32),
                pltpu.VMEM((extended, width), f32),
                pltpu.VMEM((extended, width), f32),
                pltpu.VMEM((half, width), f32),
                pltpu.VMEM((half, width), f32),
                pltpu.VMEM((2, head, width), f32),
                pltpu.VMEM((2, head, width), f32),
                pltpu.VMEM((2, head, width), f32),
                pltpu.VMEM((7, width, width), bf16),
                pltpu.VMEM((7, width, width), bf16),
                pltpu.VMEM((half, width), f32),
                pltpu.VMEM((groups, STEP, width), f32),
                pltpu.VMEM(tail_cols.shape, f32),
                dma((2, depth - 1)),
                dma((2, depth - 1)),
                dma((2, depth)),
                dma((2, depth)),
                dma((rows - 1,)),
                dma((rows - 1,)),
                dma((8,)),
                dma((8,)),
                dma((6,)),
                dma((n_all,)),
                dma((n_all,)),
                dma((n_all,)),
                dma((n_all,)),
                dma((n_data,)),
                dma((n_data,)),
                dma((n_data,)),
                dma((n_data,)),
                dma((n_data,)),
                dma((groups,)),
            ],
            compiler_params=pltpu.CompilerParams(
                collective_id=0, has_side_effects=True, vmem_limit_bytes=48 << 20
            ),
        )(*operands)

    placed = (
        P("row", "panel"),
        P("row", None),
        P(("panel", "row"), None),
        P(("panel", "row"), None),
        P(("panel", "row"), None),
        P(("row", "panel"), None),
    )
    return jax.shard_map(
        on_device,
        mesh=mesh,
        in_specs=placed,
        out_specs=(P("row", "panel"), P(("row", "panel"), None)),
        check_vma=False,
    )
```

```python
import functools

import jax
import jax.numpy as jnp
from jax import lax
from jax.experimental import pallas as pl
from jax.experimental.pallas import tpu as pltpu
from jax.sharding import PartitionSpec as P

MESH = pl.DeviceIdType.MESH
STEP = 32
GROUP = 4
NT = (((1,), (1,)), ((), ()))
NN = (((1,), (0,)), ((), ()))


def split(value):
    high = value.astype(jnp.bfloat16)
    low = (value - high.astype(jnp.float32)).astype(jnp.bfloat16)
    return high, low


def dot3(left, right, dims):
    left_high, left_low = split(left)
    right_high, right_low = split(right)
    dot = functools.partial(lax.dot_general, dimension_numbers=dims, preferred_element_type=jnp.float32)
    return dot(left_high, right_high) + (dot(left_high, right_low) + dot(left_low, right_high))


def kernel(
    panels, rows,
    slab, boundary, inverse_ref, beneath_ref, coupling_ref, cols_ref,
    factor_ref, tail_ref,
    slabs, inverses, beneath, couplings, products, constants, offset, entering, solved,
    sums_in, sums_out, inflow, passed, carry, carry_even, carry_sum, fixed, weight_high, weight_low, share, total, cols,
    z_send, z_recv, x_send, x_recv, g_send, g_recv, k_send, k_recv, f_send, f_recv, pair_send, pair_recv, local_sem,
    y_send, y_recv, t_send, t_recv, in_send, in_recv, lead_send, relay_send, u_send, u_recv,
):
    p, r = lax.axis_index("panel"), lax.axis_index("row")
    core = lax.rem(p, 2)
    chip = lax.div(p, 2)
    chips = panels // 2
    groups = chips // GROUP
    group, spot = lax.div(chip, GROUP), lax.rem(chip, GROUP)
    side = lax.div(p, panels // 2)
    z, x = lax.div(r, 2), lax.rem(r, 2)
    depth = rows // 2
    half = slab.shape[0] // 2
    width = slab.shape[1]
    head = width // 2
    n_head, n_data = head // STEP, half // STEP
    n_all = n_head + n_data
    n_sum = 1 + n_data
    piece = head // rows
    body = pl.ds(head, half)
    mine = pl.ds(pl.multiple_of(core * half, half), half)
    other = pl.ds(pl.multiple_of((1 - core) * half, half), half)
    steps = sorted(range(1, depth), key=lambda d: (-min(d, depth - d), d))

    first, final = spot == 0, spot == GROUP - 1
    carried = group > 0
    feeds = final & (group < groups - 1)

    def at(panel):
        return {"panel": panel, "row": r}

    sibling = at(p + 1 - 2 * core)
    beside = {"panel": p, "row": r + 1 - 2 * x}
    after, ahead = at(p + 2), at(p - 2)
    skip_after, skip_ahead = at(p + 2 * GROUP), at(p - 2 * GROUP)
    source_panels = [2 * (GROUP * k + GROUP - 1) for k in range(groups)]

    def z_row(shift):
        return lax.rem(z + shift + depth, depth) * 2 + x

    def any_row(shift):
        return lax.rem(r + shift + rows, rows)

    local_slab = pltpu.make_async_copy(slab.at[mine], slabs.at[core], local_sem.at[0])
    local_slab.start()
    local_cols = pltpu.make_async_copy(cols_ref, cols, local_sem.at[1])
    local_cols.start()
    local_boundary = pltpu.make_async_copy(boundary.at[mine], entering.at[body], local_sem.at[2])

    @pl.when(chip == 0)
    def _():
        local_boundary.start()

    full = (inverses.at[core], beneath, couplings.at[core])
    shards = (inverse_ref, beneath_ref, coupling_ref)
    local_shards = [pltpu.make_async_copy(shards[k], full[k].at[r], local_sem.at[3 + k]) for k in range(3)]
    for copy in local_shards:
        copy.start()

    barrier = pltpu.get_barrier_semaphore()

    def greet(target):
        pl.semaphore_signal(barrier, inc=1, device_id=target, device_id_type=MESH)

    for shift in range(1, rows):
        greet({"panel": p, "row": any_row(shift)})
    greet(sibling)

    @pl.when(chip > 0)
    def _():
        greet(ahead)

    @pl.when(final & carried)
    def _():
        greet(skip_ahead)

    for start in source_panels:
        @pl.when(start + side != p)
        def _():
            greet(at(start + side))

    expected = (
        rows + jnp.where(chip < chips - 1, 1, 0) + jnp.where(feeds, 1, 0)
        + jnp.where(final, jnp.where(side == core, n_data - 1, n_data), 0)
    )
    pl.semaphore_wait(barrier, expected)

    def remote(src, dst, send, recv, target):
        return pltpu.make_async_remote_copy(
            src_ref=src, dst_ref=dst, send_sem=send, recv_sem=recv, device_id=target, device_id_type=MESH
        )

    def z_copy(k, i, shift, place):
        return remote(
            shards[k], full[k].at[place], z_send.at[k, i], z_recv.at[k, i], {"panel": p, "row": z_row(shift)}
        )

    def x_own(k):
        return remote(shards[k], full[k].at[r], x_send.at[k, depth - 1], x_recv.at[k, depth - 1], beside)

    def x_relay(k, i, shift):
        place = full[k].at[z_row(-shift)]
        return remote(place, place, x_send.at[k, i], x_recv.at[k, i], beside)

    def g_copy(shift, place):
        return remote(
            shards[2], full[2].at[place], g_send.at[shift - 1], g_recv.at[shift - 1],
            {"panel": p, "row": any_row(shift)},
        )

    def to_sibling(k, src, dst):
        return remote(src, dst, pair_send.at[k], pair_recv.at[k], sibling)

    pair_slab = to_sibling(0, slab.at[other], slabs.at[core])
    pair_inverse = to_sibling(1, inverses.at[core], inverses.at[core])
    pair_product = to_sibling(2, products.at[core], products.at[core])
    pair_coupling = to_sibling(3, couplings.at[core], couplings.at[core])
    pair_carry = to_sibling(4, solved.at[1, pl.ds(0, head)], carry.at[core])
    pair_even = to_sibling(5, solved.at[0, pl.ds(0, head)], carry_even.at[core])
    pair_sum = to_sibling(6, carry_sum.at[core], carry_sum.at[core])

    for k in range(2):
        x_own(k).start()
        for i, shift in enumerate(steps):
            z_copy(k, i, shift, r).start()
        if k == 0:
            pair_slab.start()
    for copy in local_shards:
        copy.wait()

    def relay(k):
        for i, shift in enumerate(steps):
            z_copy(k, i, shift, z_row(-shift)).wait_recv()
            x_relay(k, i, shift).start()

    def x_arrivals(k):
        x_own(k).wait_recv()
        for i, shift in enumerate(steps):
            x_relay(k, i, shift).wait_recv()

    def square(ref):
        return ref[...].reshape(width, width)

    def keep(k, value):
        weight_high[k], weight_low[k] = split(value)

    def times(value, k):
        high, low = split(value)
        count = value.shape[0]
        both = jnp.dot(jnp.concatenate([high, low], axis=0), weight_high[k], preferred_element_type=jnp.float32)
        rest = jnp.dot(high, weight_low[k], preferred_element_type=jnp.float32)
        return both[:count] + (both[count:] + rest)

    zeros = jnp.zeros((head, width), jnp.float32)
    offset[:head] = zeros
    constants[0, :head] = zeros

    @pl.when(first)
    def _():
        row = lax.broadcasted_iota(jnp.int32, (head, width), 0) + core * head
        column = lax.broadcasted_iota(jnp.int32, (head, width), 1)
        entering[:head] = jnp.where(row == column, 1.0, 0.0)

    @pl.when(first & carried)
    def _():
        entering[body] = jnp.zeros((half, width), jnp.float32)

    relay(0)
    relay(1)
    for shift in range(1, rows):
        g_copy(shift, r).start()
    x_arrivals(0)
    pair_inverse.start()
    x_arrivals(1)
    products[core] = dot3(square(inverses.at[core]), square(beneath), NN)
    pair_product.start()
    local_slab.wait()
    constants[core, body] = dot3(slabs[core], square(inverses.at[core]), NT)
    pair_slab.wait_recv()
    pair_inverse.wait_recv()
    constants[1 - core, body] = dot3(slabs[1 - core], square(inverses.at[1 - core]), NT)
    pair_product.wait_recv()
    keep(0, dot3(products[1], products[0], NN).T)
    offset[body] = constants[1, body] - dot3(constants[0, body], products[1], NT)
    keep(1, products[0].T)

    @pl.when(chip == 0)
    def _():
        local_boundary.wait()

    def batch(b):
        return pl.ds(pl.multiple_of(b * STEP, STEP), STEP)

    def data(b):
        return pl.ds(pl.multiple_of(b * STEP + head, STEP), STEP)

    def y_copy(b):
        return remote(solved.at[1, batch(b)], entering.at[batch(b)], y_send.at[b], y_recv.at[b], after)

    def part_of(row):
        return pl.ds(pl.multiple_of(row * piece, piece), piece)

    def t_copy(b, place):
        return remote(sums_out.at[place], sums_in.at[place], t_send.at[b], t_recv.at[b], after)

    def k_copy(shift, place):
        return remote(
            sums_out.at[part_of(r)], carry_sum.at[core, place], k_send.at[shift - 1], k_recv.at[shift - 1],
            {"panel": p, "row": any_row(shift)},
        )

    def factor_copy(b):
        place = pl.ds(pl.multiple_of(core * half + b * STEP, STEP), STEP)
        return remote(solved.at[1 - core, data(b)], factor_ref.at[place], f_send.at[b], f_recv.at[b], sibling)

    def hand_in(b):
        place = pl.ds(pl.multiple_of(core * half + b * STEP, STEP), STEP)
        factor_copy(b).start()
        factor_ref[place] = solved[core, data(b)]

    def in_copy(b):
        return remote(passed.at[batch(b)], inflow.at[batch(b)], in_send.at[b], in_recv.at[b], skip_after)

    def lead_copy(b):
        return remote(passed.at[batch(b)], inflow.at[batch(b)], lead_send.at[b], in_recv.at[b], after)

    def relay_copy(b):
        return remote(inflow.at[batch(b)], inflow.at[batch(b)], relay_send.at[b], in_recv.at[b], after)

    def u_copy(b):
        return remote(
            share.at[batch(b)], total.at[group], u_send.at[b], u_recv.at[group], at(core * n_data + b)
        )

    begin = jnp.where(carried, 0, n_head)
    couple_turn = jnp.where(final, 8, n_all - 4)
    fix_turn = jnp.where(final, 12, n_all)
    relays = carried & (spot < GROUP - 2)
    fills = carried & (spot < GROUP - 1)
    inflow_lag = jnp.where(final, 8 * group, n_all + n_sum + 1)
    sum_lag = n_all
    share_lag = jnp.where(carried, sum_lag + 13, sum_lag + 2)
    turns = n_all + n_sum + 1 + n_data

    def turn(i, unused):
        @pl.when((i >= begin) & (i < n_all))
        def _():
            @pl.when(spot > 0)
            def _():
                y_copy(i).wait_recv()

            row = offset[batch(i)] + times(entering[batch(i)], 0)
            solved[1, batch(i)] = row

            @pl.when(spot < GROUP - 1)
            def _():
                y_copy(i).start()

            @pl.when(final & (group == 0))
            def _():
                passed[batch(i - n_head)] = row
                in_copy(i - n_head).start()
                lead_copy(i - n_head).start()

        @pl.when(carried & (i == n_head))
        def _():
            pair_carry.start()
            carry[core] = solved[1, :head]

        @pl.when(i == couple_turn)
        def _():
            for shift in range(1, rows):
                g_copy(shift, any_row(-shift)).wait_recv()
            pair_coupling.start()

        @pl.when(i == fix_turn)
        def _():
            pair_coupling.wait_recv()
            keep(2, square(couplings.at[0]))
            keep(3, square(couplings.at[1]))

        @pl.when(final & (i == fix_turn))
        def _():
            step = weight_high[0].astype(jnp.float32) + weight_low[0].astype(jnp.float32)
            keep(7, times(step, 3) - times(products[0].T, 2))
            fixed[...] = times(constants[0, body], 2) + times(offset[body], 3)

        b = i - sum_lag

        def add_up(place, part):
            @pl.when(first)
            def _():
                sums_out[place] = part

            @pl.when(spot > 0)
            def _():
                t_copy(b, place).wait_recv()
                sums_out[place] = sums_in[place] + part

            @pl.when(spot < GROUP - 1)
            def _():
                t_copy(b, place).start()

        @pl.when(carried & (b == 0))
        def _():
            place = part_of(r)
            solved[0, :head] = -times(entering[:head], 1)
            add_up(place, times(solved[0, place], 2) + times(solved[1, place], 3))
            pair_even.start()
            carry_even[core] = solved[0, :head]

        @pl.when((b > 0) & (b < n_sum) & (spot < GROUP - 1))
        def _():
            place = data(b - 1)
            even = constants[0, place] - times(entering[place], 1)
            solved[0, place] = even
            add_up(place, times(even, 2) + times(solved[1, place], 3))

        @pl.when((b > 0) & (b < n_sum) & final)
        def _():
            place = data(b - 1)
            add_up(place, fixed[batch(b - 1)] + times(entering[place], 7))

        @pl.when(carried & final & (b == 0))
        def _():
            carry_sum[core, part_of(r)] = sums_out[part_of(r)]
            for shift in range(1, rows):
                k_copy(shift, part_of(r)).start()

        @pl.when(carried & final & (i == share_lag - 3))
        def _():
            for shift in range(1, rows):
                k_copy(shift, part_of(any_row(-shift))).wait_recv()
            pair_sum.start()

        @pl.when(fills & (i == inflow_lag))
        def _():
            def sent(k, unused):
                y_copy(k).wait_send()
                return unused

            lax.fori_loop(begin, n_all, sent, 0)
            pair_carry.wait_recv()
            keep(4, carry[...].reshape(width, width))
            pair_even.wait_recv()
            keep(5, carry_even[...].reshape(width, width))

        @pl.when(carried & final & (i == inflow_lag))
        def _():
            pair_carry.wait_recv()
            keep(4, carry[...].reshape(width, width))

        m = i - inflow_lag

        @pl.when(carried & (m >= 0) & (m < n_data))
        def _():
            in_copy(m).wait_recv()

            @pl.when(relays)
            def _():
                relay_copy(m).start()

            @pl.when(spot < GROUP - 1)
            def _():
                value = inflow[batch(m)]
                solved[1, data(m)] += times(value, 4)
                solved[0, data(m)] += times(value, 5)
                hand_in(m)

            @pl.when(final)
            def _():
                passed[batch(m)] = solved[1, data(m)] + times(inflow[batch(m)], 4)

            @pl.when(feeds)
            def _():
                in_copy(m).start()
                lead_copy(m).start()

        @pl.when(carried & final & (i == share_lag))
        def _():
            pair_sum.wait_recv()
            keep(6, carry_sum[...].reshape(width, width))

        t = i - share_lag

        @pl.when(final & (t >= 0) & (t < n_data))
        def _():
            @pl.when(carried)
            def _():
                share[batch(t)] = sums_out[data(t)] + times(inflow[batch(t)], 6)

            @pl.when(group == 0)
            def _():
                share[batch(t)] = sums_out[data(t)]

            @pl.when(core * n_data + t != p)
            def _():
                u_copy(t).start()

            @pl.when(core * n_data + t == p)
            def _():
                total[group] = share[batch(t)]

        return unused

    lax.fori_loop(0, turns, turn, 0)

    @pl.when(final & carried)
    def _():
        solved[1, body] = passed[...]

    @pl.when(spot < GROUP - 1)
    def _():
        @pl.when(group == 0)
        def _():
            def sent(k, unused):
                y_copy(k).wait_send()
                return unused

            lax.fori_loop(begin, n_all, sent, 0)

        @pl.when(carried)
        def _():
            t_copy(0, part_of(r)).wait_send()

        def summed_up(k, unused):
            t_copy(k, data(k - 1)).wait_send()
            return unused

        lax.fori_loop(1, n_sum, summed_up, 0)

    @pl.when(final)
    def _():
        solved[0, body] = constants[0, body] - times(entering[body], 1)

    @pl.when(final & carried)
    def _():
        pair_even.wait_recv()
        keep(5, carry_even[...].reshape(width, width))
        solved[0, body] += times(inflow[...], 5)

    @pl.when(jnp.logical_not(fills))
    def _():
        def hand_all(k, unused):
            hand_in(k)
            return unused

        lax.fori_loop(0, n_data, hand_all, 0)

    for k, start in enumerate(source_panels):
        @pl.when(start + side != p)
        def _():
            remote(share.at[batch(0)], total.at[k], u_send.at[0], u_recv.at[k], at(start + side)).wait_recv()

    local_cols.wait()
    summed = total[0]
    for k in range(1, groups):
        summed = summed + total[k]
    tail_ref[...] = cols[...] - summed

    def drain(b, unused):
        factor_copy(b).wait()

        @pl.when(feeds)
        def _():
            in_copy(b).wait_send()
            lead_copy(b).wait_send()

        @pl.when(relays)
        def _():
            relay_copy(b).wait_send()

        @pl.when(final & (core * n_data + b != p))
        def _():
            u_copy(b).wait_send()

        return unused

    lax.fori_loop(0, n_data, drain, 0)

    for k in range(2):
        x_own(k).wait_send()
        for i, shift in enumerate(steps):
            z_copy(k, i, shift, r).wait_send()
            x_relay(k, i, shift).wait_send()
    for shift in range(1, rows):
        g_copy(shift, r).wait_send()
    pair_slab.wait_send()
    pair_inverse.wait_send()
    pair_product.wait_send()
    pair_coupling.wait_send()

    @pl.when(carried)
    def _():
        pair_carry.wait_send()
        pair_even.wait_send()

    @pl.when(carried & final)
    def _():
        pair_sum.wait_send()
        for shift in range(1, rows):
            k_copy(shift, part_of(r)).wait_send()


def solution(mesh):
    panels, rows = mesh.shape["panel"], mesh.shape["row"]

    def on_device(slab, boundary, diag_inverse, sub_block, tail_coupling, tail_cols):
        height, width = slab.shape
        half, head = height // 2, width // 2
        extended = head + half
        depth = rows // 2
        n_data, n_all = half // STEP, extended // STEP
        groups = panels // 2 // GROUP
        f32, bf16 = jnp.float32, jnp.bfloat16
        shard = diag_inverse.shape[0]
        whole = pl.BlockSpec(memory_space=pltpu.VMEM)
        apart = pl.BlockSpec(memory_space=pltpu.HBM)
        dma = pltpu.SemaphoreType.DMA
        operands = [
            pltpu.with_memory_space_constraint(value, pltpu.HBM)
            for value in (slab, boundary, diag_inverse, sub_block, tail_coupling, tail_cols)
        ]
        return pl.pallas_call(
            functools.partial(kernel, panels, rows),
            out_shape=(
                jax.ShapeDtypeStruct((height, width), f32),
                jax.ShapeDtypeStruct(tail_cols.shape, f32),
            ),
            in_specs=[apart] * 6,
            out_specs=(whole, whole),
            scratch_shapes=[
                pltpu.VMEM((2, half, width), f32),
                pltpu.VMEM((2, rows, shard, width), f32),
                pltpu.VMEM((rows, shard, width), f32),
                pltpu.VMEM((2, rows, shard, width), f32),
                pltpu.VMEM((2, width, width), f32),
                pltpu.VMEM((2, extended, width), f32),
                pltpu.VMEM((extended, width), f32),
                pltpu.VMEM((extended, width), f32),
                pltpu.VMEM((2, extended, width), f32),
                pltpu.VMEM((extended, width), f32),
                pltpu.VMEM((extended, width), f32),
                pltpu.VMEM((half, width), f32),
                pltpu.VMEM((half, width), f32),
                pltpu.VMEM((2, head, width), f32),
                pltpu.VMEM((2, head, width), f32),
                pltpu.VMEM((2, head, width), f32),
                pltpu.VMEM((half, width), f32),
                pltpu.VMEM((8, width, width), bf16),
                pltpu.VMEM((8, width, width), bf16),
                pltpu.VMEM((half, width), f32),
                pltpu.VMEM((groups, STEP, width), f32),
                pltpu.VMEM(tail_cols.shape, f32),
                dma((2, depth - 1)),
                dma((2, depth - 1)),
                dma((2, depth)),
                dma((2, depth)),
                dma((rows - 1,)),
                dma((rows - 1,)),
                dma((rows - 1,)),
                dma((rows - 1,)),
                dma((n_data,)),
                dma((n_data,)),
                dma((7,)),
                dma((7,)),
                dma((6,)),
                dma((n_all,)),
                dma((n_all,)),
                dma((n_all,)),
                dma((n_all,)),
                dma((n_data,)),
                dma((n_data,)),
                dma((n_data,)),
                dma((n_data,)),
                dma((n_data,)),
                dma((groups,)),
            ],
            compiler_params=pltpu.CompilerParams(
                collective_id=0, has_side_effects=True, vmem_limit_bytes=48 << 20
            ),
        )(*operands)

    placed = (
        P("row", "panel"),
        P("row", None),
        P(("panel", "row"), None),
        P(("panel", "row"), None),
        P(("panel", "row"), None),
        P(("row", "panel"), None),
    )
    return jax.shard_map(
        on_device,
        mesh=mesh,
        in_specs=placed,
        out_specs=(P("row", "panel"), P(("row", "panel"), None)),
        check_vma=False,
    )
```

```python
import functools

import jax
import jax.numpy as jnp
from jax import lax
from jax.experimental import pallas as pl
from jax.experimental.pallas import tpu as pltpu
from jax.sharding import PartitionSpec as P

MESH = pl.DeviceIdType.MESH
STEP = 32
GROUP = 4
NT = (((1,), (1,)), ((), ()))
NN = (((1,), (0,)), ((), ()))


def split(value):
    high = value.astype(jnp.bfloat16)
    low = (value - high.astype(jnp.float32)).astype(jnp.bfloat16)
    return high, low


def dot3(left, right, dims):
    left_high, left_low = split(left)
    right_high, right_low = split(right)
    dot = functools.partial(lax.dot_general, dimension_numbers=dims, preferred_element_type=jnp.float32)
    return dot(left_high, right_high) + (dot(left_high, right_low) + dot(left_low, right_high))


def kernel(
    panels, rows,
    slab, boundary, inverse_ref, beneath_ref, coupling_ref, cols_ref,
    factor_ref, tail_ref,
    slabs, inverses, beneath, couplings, products, constants, offset, entering, solved,
    sums_in, sums_out, inflow, passed, carry, carry_even, carry_sum, fixed, weight_high, weight_low, share, total, cols,
    z_send, z_recv, x_send, x_recv, g_send, g_recv, k_send, k_recv, f_send, f_recv, pair_send, pair_recv, local_sem,
    y_send, y_recv, t_send, t_recv, in_send, in_recv, lead_send, relay_send, u_send, u_recv,
):
    p, r = lax.axis_index("panel"), lax.axis_index("row")
    core = lax.rem(p, 2)
    chip = lax.div(p, 2)
    chips = panels // 2
    groups = chips // GROUP
    group, spot = lax.div(chip, GROUP), lax.rem(chip, GROUP)
    side = lax.div(p, panels // 2)
    z, x = lax.div(r, 2), lax.rem(r, 2)
    depth = rows // 2
    half = slab.shape[0] // 2
    width = slab.shape[1]
    head = width // 2
    n_head, n_data = head // STEP, half // STEP
    n_all = n_head + n_data
    n_sum = 1 + n_data
    piece = head // rows
    body = pl.ds(head, half)
    mine = pl.ds(pl.multiple_of(core * half, half), half)
    other = pl.ds(pl.multiple_of((1 - core) * half, half), half)
    steps = sorted(range(1, depth), key=lambda d: (-min(d, depth - d), d))

    first, final = spot == 0, spot == GROUP - 1
    carried = group > 0
    feeds = final & (group < groups - 1)

    def at(panel):
        return {"panel": panel, "row": r}

    sibling = at(p + 1 - 2 * core)
    beside = {"panel": p, "row": r + 1 - 2 * x}
    after, ahead = at(p + 2), at(p - 2)
    skip_after, skip_ahead = at(p + 2 * GROUP), at(p - 2 * GROUP)
    source_panels = [2 * (GROUP * k + GROUP - 1) for k in range(groups)]

    def z_row(shift):
        return lax.rem(z + shift + depth, depth) * 2 + x

    def any_row(shift):
        return lax.rem(r + shift + rows, rows)

    local_slab = pltpu.make_async_copy(slab.at[mine], slabs.at[core], local_sem.at[0])
    local_slab.start()
    local_cols = pltpu.make_async_copy(cols_ref, cols, local_sem.at[1])
    local_cols.start()
    local_boundary = pltpu.make_async_copy(boundary.at[mine], entering.at[body], local_sem.at[2])

    @pl.when(chip == 0)
    def _():
        local_boundary.start()

    full = (inverses.at[core], beneath, couplings.at[core])
    shards = (inverse_ref, beneath_ref, coupling_ref)
    local_shards = [pltpu.make_async_copy(shards[k], full[k].at[r], local_sem.at[3 + k]) for k in range(3)]
    for copy in local_shards:
        copy.start()

    barrier = pltpu.get_barrier_semaphore()

    def greet(target):
        pl.semaphore_signal(barrier, inc=1, device_id=target, device_id_type=MESH)

    for shift in range(1, rows):
        greet({"panel": p, "row": any_row(shift)})
    greet(sibling)

    @pl.when(chip > 0)
    def _():
        greet(ahead)

    @pl.when(final & carried)
    def _():
        greet(skip_ahead)

    for start in source_panels:
        @pl.when(start + side != p)
        def _():
            greet(at(start + side))

    expected = (
        rows + jnp.where(chip < chips - 1, 1, 0) + jnp.where(feeds, 1, 0)
        + jnp.where(final, jnp.where(side == core, n_data - 1, n_data), 0)
    )
    pl.semaphore_wait(barrier, expected)

    def remote(src, dst, send, recv, target):
        return pltpu.make_async_remote_copy(
            src_ref=src, dst_ref=dst, send_sem=send, recv_sem=recv, device_id=target, device_id_type=MESH
        )

    def z_copy(k, i, shift, place):
        return remote(
            shards[k], full[k].at[place], z_send.at[0], z_recv.at[k, i], {"panel": p, "row": z_row(shift)}
        )

    def x_own(k):
        return remote(shards[k], full[k].at[r], x_send.at[0], x_recv.at[k], beside)

    def x_relay(k, i, shift):
        place = full[k].at[z_row(-shift)]
        return remote(place, place, x_send.at[0], x_recv.at[k], beside)

    def g_copy(shift, place):
        return remote(
            shards[2], full[2].at[place], g_send.at[0], g_recv.at[0],
            {"panel": p, "row": any_row(shift)},
        )

    def to_sibling(k, src, dst):
        return remote(src, dst, pair_send.at[k], pair_recv.at[k], sibling)

    pair_slab = to_sibling(0, slab.at[other], slabs.at[core])
    pair_inverse = to_sibling(1, inverses.at[core], inverses.at[core])
    pair_product = to_sibling(2, products.at[core], products.at[core])
    pair_coupling = to_sibling(3, couplings.at[core], couplings.at[core])
    pair_carry = to_sibling(4, solved.at[1, pl.ds(0, head)], carry.at[core])
    pair_even = to_sibling(5, solved.at[0, pl.ds(0, head)], carry_even.at[core])
    pair_sum = to_sibling(6, carry_sum.at[core], carry_sum.at[core])

    for k in range(2):
        x_own(k).start()
        for i, shift in enumerate(steps):
            z_copy(k, i, shift, r).start()
        if k == 0:
            pair_slab.start()
    for copy in local_shards:
        copy.wait()

    def relay(k):
        for i, shift in enumerate(steps):
            z_copy(k, i, shift, z_row(-shift)).wait_recv()
            x_relay(k, i, shift).start()

    def sent(ref, sem):
        remote(ref, ref, sem.at[0], sem.at[0], sibling).wait_send()

    def received(ref, sem):
        remote(ref, ref, sem, sem, sibling).wait_recv()

    def x_arrivals(k):
        received(full[k].at[pl.ds(0, depth)], x_recv.at[k])

    def square(ref):
        return ref[...].reshape(width, width)

    def keep(k, value):
        weight_high[k], weight_low[k] = split(value)

    def times(value, k):
        high, low = split(value)
        count = value.shape[0]
        both = jnp.dot(jnp.concatenate([high, low], axis=0), weight_high[k], preferred_element_type=jnp.float32)
        rest = jnp.dot(high, weight_low[k], preferred_element_type=jnp.float32)
        return both[:count] + (both[count:] + rest)

    zeros = jnp.zeros((head, width), jnp.float32)
    offset[:head] = zeros
    constants[0, :head] = zeros

    @pl.when(first)
    def _():
        row = lax.broadcasted_iota(jnp.int32, (head, width), 0) + core * head
        column = lax.broadcasted_iota(jnp.int32, (head, width), 1)
        entering[:head] = jnp.where(row == column, 1.0, 0.0)

    @pl.when(first & carried)
    def _():
        entering[body] = jnp.zeros((half, width), jnp.float32)

    relay(0)
    relay(1)
    for shift in range(1, rows):
        g_copy(shift, r).start()
    x_arrivals(0)
    pair_inverse.start()
    x_arrivals(1)
    products[core] = dot3(square(inverses.at[core]), square(beneath), NN)
    pair_product.start()
    local_slab.wait()
    constants[core, body] = dot3(slabs[core], square(inverses.at[core]), NT)
    pair_slab.wait_recv()
    pair_inverse.wait_recv()
    constants[1 - core, body] = dot3(slabs[1 - core], square(inverses.at[1 - core]), NT)
    pair_product.wait_recv()
    keep(0, dot3(products[1], products[0], NN).T)
    offset[body] = constants[1, body] - dot3(constants[0, body], products[1], NT)
    keep(1, products[0].T)

    @pl.when(chip == 0)
    def _():
        local_boundary.wait()

    def batch(b):
        return pl.ds(pl.multiple_of(b * STEP, STEP), STEP)

    def data(b):
        return pl.ds(pl.multiple_of(b * STEP + head, STEP), STEP)

    def y_copy(b):
        return remote(solved.at[1, batch(b)], entering.at[batch(b)], y_send.at[0], y_recv.at[b], after)

    def part_of(row):
        return pl.ds(pl.multiple_of(row * piece, piece), piece)

    def t_copy(b, place):
        return remote(sums_out.at[place], sums_in.at[place], t_send.at[0], t_recv.at[b], after)

    def k_copy(shift, place):
        return remote(
            sums_out.at[part_of(r)], carry_sum.at[core, place], k_send.at[0], k_recv.at[0],
            {"panel": p, "row": any_row(shift)},
        )

    def factor_copy(b):
        place = pl.ds(pl.multiple_of(core * half + b * STEP, STEP), STEP)
        return remote(solved.at[1 - core, data(b)], factor_ref.at[place], f_send.at[0], f_recv.at[0], sibling)

    def hand_in(b):
        place = pl.ds(pl.multiple_of(core * half + b * STEP, STEP), STEP)
        factor_copy(b).start()
        factor_ref[place] = solved[core, data(b)]

    def in_copy(b):
        return remote(passed.at[batch(b)], inflow.at[batch(b)], in_send.at[0], in_recv.at[b], skip_after)

    def lead_copy(b):
        return remote(passed.at[batch(b)], inflow.at[batch(b)], lead_send.at[0], in_recv.at[b], after)

    def relay_copy(b):
        return remote(inflow.at[batch(b)], inflow.at[batch(b)], relay_send.at[0], in_recv.at[b], after)

    def u_copy(b):
        return remote(
            share.at[batch(b)], total.at[group], u_send.at[0], u_recv.at[group], at(core * n_data + b)
        )

    begin = jnp.where(carried, 0, n_head)
    couple_turn = jnp.where(final, 8, n_all - 4)
    fix_turn = jnp.where(final, 12, n_all)
    relays = carried & (spot < GROUP - 2)
    fills = carried & (spot < GROUP - 1)
    inflow_lag = jnp.where(final, 8 * group, n_all + n_sum + 1)
    sum_lag = n_all
    share_lag = jnp.where(carried, sum_lag + 13, sum_lag + 9)
    turns = n_all + n_sum + 1 + n_data

    def turn(i, unused):
        @pl.when((i >= begin) & (i < n_all))
        def _():
            @pl.when(spot > 0)
            def _():
                y_copy(i).wait_recv()

            row = offset[batch(i)] + times(entering[batch(i)], 0)
            solved[1, batch(i)] = row

            @pl.when(spot < GROUP - 1)
            def _():
                y_copy(i).start()

            @pl.when(final & (group == 0))
            def _():
                passed[batch(i - n_head)] = row
                in_copy(i - n_head).start()
                lead_copy(i - n_head).start()

        @pl.when(carried & (i == n_head))
        def _():
            pair_carry.start()
            carry[core] = solved[1, :head]

        @pl.when(i == couple_turn)
        def _():
            received(couplings.at[core, pl.ds(0, rows - 1)], g_recv.at[0])
            pair_coupling.start()

        @pl.when(i == fix_turn)
        def _():
            pair_coupling.wait_recv()
            keep(2, square(couplings.at[0]))
            keep(3, square(couplings.at[1]))

        @pl.when(final & (i == fix_turn))
        def _():
            step = weight_high[0].astype(jnp.float32) + weight_low[0].astype(jnp.float32)
            keep(7, times(step, 3) - times(products[0].T, 2))
            fixed[...] = times(constants[0, body], 2) + times(offset[body], 3)

        b = i - sum_lag

        def add_up(place, part):
            @pl.when(first)
            def _():
                sums_out[place] = part

            @pl.when(spot > 0)
            def _():
                t_copy(b, place).wait_recv()
                sums_out[place] = sums_in[place] + part

            @pl.when(spot < GROUP - 1)
            def _():
                t_copy(b, place).start()

        @pl.when(carried & (b == 0))
        def _():
            place = part_of(r)
            solved[0, :head] = -times(entering[:head], 1)
            add_up(place, times(solved[0, place], 2) + times(solved[1, place], 3))
            pair_even.start()
            carry_even[core] = solved[0, :head]

        @pl.when((b > 0) & (b < n_sum) & (spot < GROUP - 1))
        def _():
            place = data(b - 1)
            even = constants[0, place] - times(entering[place], 1)
            solved[0, place] = even
            add_up(place, times(even, 2) + times(solved[1, place], 3))

        @pl.when((b > 0) & (b < n_sum) & final)
        def _():
            place = data(b - 1)
            add_up(place, fixed[batch(b - 1)] + times(entering[place], 7))

        @pl.when(carried & final & (b == 0))
        def _():
            carry_sum[core, part_of(r)] = sums_out[part_of(r)]
            for shift in range(1, rows):
                k_copy(shift, part_of(r)).start()

        @pl.when(carried & final & (i == share_lag - 3))
        def _():
            received(carry_sum.at[core, pl.ds(0, (rows - 1) * piece)], k_recv.at[0])
            pair_sum.start()

        @pl.when(fills & (i == inflow_lag))
        def _():
            sent(entering, y_send)
            pair_carry.wait_recv()
            keep(4, carry[...].reshape(width, width))
            pair_even.wait_recv()
            keep(5, carry_even[...].reshape(width, width))

        @pl.when(carried & final & (i == inflow_lag))
        def _():
            pair_carry.wait_recv()
            keep(4, carry[...].reshape(width, width))

        m = i - inflow_lag

        @pl.when(carried & (m >= 0) & (m < n_data))
        def _():
            in_copy(m).wait_recv()

            @pl.when(relays)
            def _():
                relay_copy(m).start()

            @pl.when(spot < GROUP - 1)
            def _():
                value = inflow[batch(m)]
                solved[1, data(m)] += times(value, 4)
                solved[0, data(m)] += times(value, 5)
                hand_in(m)

            @pl.when(final)
            def _():
                passed[batch(m)] = solved[1, data(m)] + times(inflow[batch(m)], 4)

            @pl.when(feeds)
            def _():
                in_copy(m).start()
                lead_copy(m).start()

        @pl.when(carried & final & (i == share_lag))
        def _():
            pair_sum.wait_recv()
            keep(6, carry_sum[...].reshape(width, width))

        t = i - share_lag

        @pl.when(final & (t >= 0) & (t < n_data // 2))
        def _():
            pair = pl.ds(pl.multiple_of(t * 2 * STEP, 2 * STEP), 2 * STEP)
            below = pl.ds(pl.multiple_of(t * 2 * STEP + head, 2 * STEP), 2 * STEP)

            @pl.when(carried)
            def _():
                share[pair] = sums_out[below] + times(inflow[pair], 6)

            @pl.when(group == 0)
            def _():
                share[pair] = sums_out[below]

            for b in (2 * t, 2 * t + 1):
                @pl.when(core * n_data + b != p)
                def _():
                    u_copy(b).start()

                @pl.when(core * n_data + b == p)
                def _():
                    total[group] = share[batch(b)]

        return unused

    lax.fori_loop(0, turns, turn, 0)

    @pl.when(final & carried)
    def _():
        solved[1, body] = passed[...]

    @pl.when(spot < GROUP - 1)
    def _():
        @pl.when(group == 0)
        def _():
            sent(entering.at[body], y_send)
            sent(sums_in.at[body], t_send)

        @pl.when(carried)
        def _():
            sent(sums_in.at[pl.ds(0, piece + half)], t_send)

    @pl.when(final)
    def _():
        solved[0, body] = constants[0, body] - times(entering[body], 1)

    @pl.when(final & carried)
    def _():
        pair_even.wait_recv()
        keep(5, carry_even[...].reshape(width, width))
        solved[0, body] += times(inflow[...], 5)

    @pl.when(jnp.logical_not(fills))
    def _():
        def hand_all(k, unused):
            hand_in(k)
            return unused

        lax.fori_loop(0, n_data, hand_all, 0)

    for k, start in enumerate(source_panels):
        @pl.when(start + side != p)
        def _():
            remote(share.at[batch(0)], total.at[k], u_send.at[0], u_recv.at[k], at(start + side)).wait_recv()

    local_cols.wait()
    summed = total[0]
    for k in range(1, groups):
        summed = summed + total[k]
    tail_ref[...] = cols[...] - summed

    received(factor_ref.at[mine], f_recv.at[0])
    sent(factor_ref.at[mine], f_send)

    @pl.when(feeds)
    def _():
        sent(inflow, in_send)
        sent(inflow, lead_send)

    @pl.when(relays)
    def _():
        sent(inflow, relay_send)

    @pl.when(final & (side == core))
    def _():
        sent(share.at[pl.ds(0, half - STEP)], u_send)

    @pl.when(final & (side != core))
    def _():
        sent(share, u_send)

    sent(inverses.at[core, pl.ds(0, 2 * depth - 2)], z_send)
    sent(inverses.at[core], x_send)
    sent(couplings.at[core, pl.ds(0, rows - 1)], g_send)
    pair_slab.wait_send()
    pair_inverse.wait_send()
    pair_product.wait_send()
    pair_coupling.wait_send()

    @pl.when(carried)
    def _():
        pair_carry.wait_send()
        pair_even.wait_send()

    @pl.when(carried & final)
    def _():
        pair_sum.wait_send()
        sent(carry_sum.at[core, pl.ds(0, (rows - 1) * piece)], k_send)


def solution(mesh):
    panels, rows = mesh.shape["panel"], mesh.shape["row"]

    def on_device(slab, boundary, diag_inverse, sub_block, tail_coupling, tail_cols):
        height, width = slab.shape
        half, head = height // 2, width // 2
        extended = head + half
        depth = rows // 2
        n_data, n_all = half // STEP, extended // STEP
        groups = panels // 2 // GROUP
        f32, bf16 = jnp.float32, jnp.bfloat16
        shard = diag_inverse.shape[0]
        whole = pl.BlockSpec(memory_space=pltpu.VMEM)
        apart = pl.BlockSpec(memory_space=pltpu.HBM)
        dma = pltpu.SemaphoreType.DMA
        operands = [
            pltpu.with_memory_space_constraint(value, pltpu.HBM)
            for value in (slab, boundary, diag_inverse, sub_block, tail_coupling, tail_cols)
        ]
        return pl.pallas_call(
            functools.partial(kernel, panels, rows),
            out_shape=(
                jax.ShapeDtypeStruct((height, width), f32),
                jax.ShapeDtypeStruct(tail_cols.shape, f32),
            ),
            in_specs=[apart] * 6,
            out_specs=(whole, whole),
            scratch_shapes=[
                pltpu.VMEM((2, half, width), f32),
                pltpu.VMEM((2, rows, shard, width), f32),
                pltpu.VMEM((rows, shard, width), f32),
                pltpu.VMEM((2, rows, shard, width), f32),
                pltpu.VMEM((2, width, width), f32),
                pltpu.VMEM((2, extended, width), f32),
                pltpu.VMEM((extended, width), f32),
                pltpu.VMEM((extended, width), f32),
                pltpu.VMEM((2, extended, width), f32),
                pltpu.VMEM((extended, width), f32),
                pltpu.VMEM((extended, width), f32),
                pltpu.VMEM((half, width), f32),
                pltpu.VMEM((half, width), f32),
                pltpu.VMEM((2, head, width), f32),
                pltpu.VMEM((2, head, width), f32),
                pltpu.VMEM((2, head, width), f32),
                pltpu.VMEM((half, width), f32),
                pltpu.VMEM((8, width, width), bf16),
                pltpu.VMEM((8, width, width), bf16),
                pltpu.VMEM((half, width), f32),
                pltpu.VMEM((groups, STEP, width), f32),
                pltpu.VMEM(tail_cols.shape, f32),
                dma((1,)),
                dma((2, depth - 1)),
                dma((1,)),
                dma((2,)),
                dma((1,)),
                dma((1,)),
                dma((1,)),
                dma((1,)),
                dma((1,)),
                dma((1,)),
                dma((7,)),
                dma((7,)),
                dma((6,)),
                dma((1,)),
                dma((n_all,)),
                dma((1,)),
                dma((n_data + 1,)),
                dma((1,)),
                dma((n_data,)),
                dma((1,)),
                dma((1,)),
                dma((1,)),
                dma((groups,)),
            ],
            compiler_params=pltpu.CompilerParams(
                collective_id=0, has_side_effects=True, vmem_limit_bytes=48 << 20
            ),
        )(*operands)

    placed = (
        P("row", "panel"),
        P("row", None),
        P(("panel", "row"), None),
        P(("panel", "row"), None),
        P(("panel", "row"), None),
        P(("row", "panel"), None),
    )
    return jax.shard_map(
        on_device,
        mesh=mesh,
        in_specs=placed,
        out_specs=(P("row", "panel"), P(("row", "panel"), None)),
        check_vma=False,
    )
```

```python
import functools

import jax
import jax.numpy as jnp
from jax import lax
from jax.experimental import pallas as pl
from jax.experimental.pallas import tpu as pltpu
from jax.sharding import PartitionSpec as P

MESH = pl.DeviceIdType.MESH
STEP = 32
GROUP = 4
NT = (((1,), (1,)), ((), ()))
NN = (((1,), (0,)), ((), ()))


def split(value):
    high = value.astype(jnp.bfloat16)
    low = (value - high.astype(jnp.float32)).astype(jnp.bfloat16)
    return high, low


def dot3(left, right, dims):
    left_high, left_low = split(left)
    right_high, right_low = split(right)
    dot = functools.partial(lax.dot_general, dimension_numbers=dims, preferred_element_type=jnp.float32)
    return dot(left_high, right_high) + (dot(left_high, right_low) + dot(left_low, right_high))


def kernel(
    panels, rows,
    slab, boundary, inverse_ref, beneath_ref, coupling_ref, cols_ref,
    factor_ref, tail_ref,
    slabs, inverses, beneath, couplings, products, constants, offset, entering, solved,
    sums_in, sums_out, inflow, passed, carry, carry_even, carry_sum, fixed, weight_high, weight_low, share, total, cols,
    z_send, z_recv, x_send, x_recv, g_send, g_recv, k_send, k_recv, f_send, f_recv, pair_send, pair_recv, local_sem,
    y_send, y_recv, t_send, t_recv, in_send, in_recv, lead_send, relay_send, back_send, u_send, u_recv,
):
    p, r = lax.axis_index("panel"), lax.axis_index("row")
    core = lax.rem(p, 2)
    chip = lax.div(p, 2)
    chips = panels // 2
    groups = chips // GROUP
    group, spot = lax.div(chip, GROUP), lax.rem(chip, GROUP)
    side = lax.div(p, panels // 2)
    z, x = lax.div(r, 2), lax.rem(r, 2)
    depth = rows // 2
    half = slab.shape[0] // 2
    width = slab.shape[1]
    head = width // 2
    n_head, n_data = head // STEP, half // STEP
    n_all = n_head + n_data
    n_sum = 1 + n_data
    piece = head // rows
    body = pl.ds(head, half)
    mine = pl.ds(pl.multiple_of(core * half, half), half)
    other = pl.ds(pl.multiple_of((1 - core) * half, half), half)
    steps = sorted(range(1, depth), key=lambda d: (-min(d, depth - d), d))

    first, final = spot == 0, spot == GROUP - 1
    carried = group > 0
    feeds = final & (group < groups - 1)
    halved = group == 1

    def at(panel):
        return {"panel": panel, "row": r}

    sibling = at(p + 1 - 2 * core)
    beside = {"panel": p, "row": r + 1 - 2 * x}
    after, ahead = at(p + 2), at(p - 2)
    skip_after, skip_ahead = at(p + 2 * GROUP), at(p - 2 * GROUP)
    source_panels = [2 * (GROUP * k + GROUP - 1) for k in range(groups)]

    def z_row(shift):
        return lax.rem(z + shift + depth, depth) * 2 + x

    def any_row(shift):
        return lax.rem(r + shift + rows, rows)

    barrier = pltpu.get_barrier_semaphore()

    def greet(target):
        pl.semaphore_signal(barrier, inc=1, device_id=target, device_id_type=MESH)

    for shift in range(1, rows):
        greet({"panel": p, "row": any_row(shift)})
    greet(sibling)

    @pl.when(chip > 0)
    def _():
        greet(ahead)

    @pl.when(halved & (spot == GROUP - 2))
    def _():
        greet(after)

    @pl.when(final & carried)
    def _():
        greet(skip_ahead)

    for start in source_panels:
        @pl.when(start + side != p)
        def _():
            greet(at(start + side))

    local_slab = pltpu.make_async_copy(slab.at[mine], slabs.at[core], local_sem.at[0])
    local_slab.start()
    local_cols = pltpu.make_async_copy(cols_ref, cols, local_sem.at[1])
    local_cols.start()
    local_boundary = pltpu.make_async_copy(boundary.at[mine], entering.at[body], local_sem.at[2])

    @pl.when(chip == 0)
    def _():
        local_boundary.start()

    full = (inverses.at[core], beneath, couplings.at[core])
    shards = (inverse_ref, beneath_ref, coupling_ref)
    local_shards = [pltpu.make_async_copy(shards[k], full[k].at[r], local_sem.at[3 + k]) for k in range(3)]
    for copy in local_shards:
        copy.start()

    expected = (
        rows + jnp.where(chip < chips - 1, 1, 0) + jnp.where(feeds, 1, 0) + jnp.where(halved & final, 1, 0)
        + jnp.where(final, jnp.where(side == core, n_data - 1, n_data), 0)
    )
    pl.semaphore_wait(barrier, expected)

    def remote(src, dst, send, recv, target):
        return pltpu.make_async_remote_copy(
            src_ref=src, dst_ref=dst, send_sem=send, recv_sem=recv, device_id=target, device_id_type=MESH
        )

    def z_copy(k, i, shift, place):
        return remote(
            shards[k], full[k].at[place], z_send.at[0], z_recv.at[k, i], {"panel": p, "row": z_row(shift)}
        )

    def x_own(k):
        return remote(shards[k], full[k].at[r], x_send.at[0], x_recv.at[k], beside)

    def x_relay(k, i, shift):
        place = full[k].at[z_row(-shift)]
        return remote(place, place, x_send.at[0], x_recv.at[k], beside)

    def g_copy(shift, place):
        return remote(
            shards[2], full[2].at[place], g_send.at[0], g_recv.at[0],
            {"panel": p, "row": any_row(shift)},
        )

    def to_sibling(k, src, dst):
        return remote(src, dst, pair_send.at[k], pair_recv.at[k], sibling)

    pair_slab = to_sibling(0, slab.at[other], slabs.at[core])
    pair_inverse = to_sibling(1, inverses.at[core], inverses.at[core])
    pair_product = to_sibling(2, products.at[core], products.at[core])
    pair_coupling = to_sibling(3, couplings.at[core], couplings.at[core])
    pair_carry = to_sibling(4, solved.at[1, pl.ds(0, head)], carry.at[core])
    pair_even = to_sibling(5, solved.at[0, pl.ds(0, head)], carry_even.at[core])
    pair_sum = to_sibling(6, carry_sum.at[core], carry_sum.at[core])

    for k in range(2):
        x_own(k).start()
        for i, shift in enumerate(steps):
            z_copy(k, i, shift, r).start()
        if k == 0:
            pair_slab.start()
    for copy in local_shards:
        copy.wait()

    def relay(k):
        for i, shift in enumerate(steps):
            z_copy(k, i, shift, z_row(-shift)).wait_recv()
            x_relay(k, i, shift).start()

    def sent(ref, sem):
        remote(ref, ref, sem.at[0], sem.at[0], sibling).wait_send()

    def received(ref, sem):
        remote(ref, ref, sem, sem, sibling).wait_recv()

    def x_arrivals(k):
        received(full[k].at[pl.ds(0, depth)], x_recv.at[k])

    def square(ref):
        return ref[...].reshape(width, width)

    def keep(k, value):
        weight_high[k], weight_low[k] = split(value)

    def times(value, k):
        high, low = split(value)
        count = value.shape[0]
        both = jnp.dot(jnp.concatenate([high, low], axis=0), weight_high[k], preferred_element_type=jnp.float32)
        rest = jnp.dot(high, weight_low[k], preferred_element_type=jnp.float32)
        return both[:count] + (both[count:] + rest)

    zeros = jnp.zeros((head, width), jnp.float32)
    offset[:head] = zeros
    constants[0, :head] = zeros

    @pl.when(first)
    def _():
        row = lax.broadcasted_iota(jnp.int32, (head, width), 0) + core * head
        column = lax.broadcasted_iota(jnp.int32, (head, width), 1)
        entering[:head] = jnp.where(row == column, 1.0, 0.0)

    @pl.when(first & carried)
    def _():
        entering[body] = jnp.zeros((half, width), jnp.float32)

    relay(0)
    relay(1)
    x_arrivals(0)
    pair_inverse.start()
    local_slab.wait()
    constants[core, body] = dot3(slabs[core], square(inverses.at[core]), NT)
    pair_slab.wait_recv()
    pair_inverse.wait_recv()
    constants[1 - core, body] = dot3(slabs[1 - core], square(inverses.at[1 - core]), NT)
    x_arrivals(1)
    products[core] = dot3(square(inverses.at[core]), square(beneath), NN)
    pair_product.start()
    for shift in range(1, rows):
        g_copy(shift, r).start()
    pair_product.wait_recv()
    keep(0, dot3(products[1], products[0], NN).T)
    offset[body] = constants[1, body] - dot3(constants[0, body], products[1], NT)
    keep(1, products[0].T)

    @pl.when(chip == 0)
    def _():
        local_boundary.wait()

    def batch(b):
        return pl.ds(pl.multiple_of(b * STEP, STEP), STEP)

    def data(b):
        return pl.ds(pl.multiple_of(b * STEP + head, STEP), STEP)

    def y_copy(b):
        return remote(solved.at[1, batch(b)], entering.at[batch(b)], y_send.at[0], y_recv.at[b], after)

    def part_of(row):
        return pl.ds(pl.multiple_of(row * piece, piece), piece)

    def t_copy(b, place):
        return remote(sums_out.at[place], sums_in.at[place], t_send.at[0], t_recv.at[b], after)

    def k_copy(shift, place):
        return remote(
            sums_out.at[part_of(r)], carry_sum.at[core, place], k_send.at[0], k_recv.at[0],
            {"panel": p, "row": any_row(shift)},
        )

    def factor_copy(b):
        place = pl.ds(pl.multiple_of(core * half + b * STEP, STEP), STEP)
        return remote(solved.at[1 - core, data(b)], factor_ref.at[place], f_send.at[0], f_recv.at[0], sibling)

    def hand_in(b):
        place = pl.ds(pl.multiple_of(core * half + b * STEP, STEP), STEP)
        factor_copy(b).start()
        factor_ref[place] = solved[core, data(b)]

    def in_copy(b):
        return remote(passed.at[batch(b)], inflow.at[batch(b)], in_send.at[0], in_recv.at[b], skip_after)

    def lead_copy(b):
        return remote(passed.at[batch(b)], inflow.at[batch(b)], lead_send.at[0], in_recv.at[b], after)

    def relay_copy(b):
        return remote(inflow.at[batch(b)], inflow.at[batch(b)], relay_send.at[0], in_recv.at[b], after)

    def back_copy(b):
        return remote(inflow.at[batch(b)], inflow.at[batch(b)], back_send.at[0], in_recv.at[b], ahead)

    def u_copy(b):
        return remote(
            share.at[batch(b)], total.at[group], u_send.at[0], u_recv.at[group], at(core * n_data + b)
        )

    begin = jnp.where(carried, 0, n_head)
    couple_turn = jnp.where(final, 8, n_all - 4)
    fix_turn = jnp.where(final, 12, n_all)
    relays = carried & (spot < GROUP - 2)
    fills = carried & (spot < GROUP - 1)
    inflow_lag = jnp.where(final, 8 * group, n_all + n_sum + 1)
    sum_lag = n_all
    share_lag = jnp.where(carried, sum_lag + 13, sum_lag + 9)
    turns = n_all + n_sum + 1 + n_data

    def turn(i, unused):
        @pl.when((i >= begin) & (i < n_all))
        def _():
            @pl.when(spot > 0)
            def _():
                y_copy(i).wait_recv()

            row = offset[batch(i)] + times(entering[batch(i)], 0)
            solved[1, batch(i)] = row

            @pl.when(spot < GROUP - 1)
            def _():
                y_copy(i).start()

            @pl.when(final & (group == 0))
            def _():
                passed[batch(i - n_head)] = row
                in_copy(i - n_head).start()
                lead_copy(i - n_head).start()

        @pl.when(carried & (i == n_head))
        def _():
            pair_carry.start()
            carry[core] = solved[1, :head]

        @pl.when(i == couple_turn)
        def _():
            received(couplings.at[core, pl.ds(0, rows - 1)], g_recv.at[0])
            pair_coupling.start()

        @pl.when(i == fix_turn)
        def _():
            pair_coupling.wait_recv()
            keep(2, square(couplings.at[0]))
            keep(3, square(couplings.at[1]))

        @pl.when(final & (i == fix_turn))
        def _():
            step = weight_high[0].astype(jnp.float32) + weight_low[0].astype(jnp.float32)
            keep(7, times(step, 3) - times(products[0].T, 2))
            fixed[...] = times(constants[0, body], 2) + times(offset[body], 3)

        b = i - sum_lag

        def add_up(place, part):
            @pl.when(first)
            def _():
                sums_out[place] = part

            @pl.when(spot > 0)
            def _():
                t_copy(b, place).wait_recv()
                sums_out[place] = sums_in[place] + part

            @pl.when(spot < GROUP - 1)
            def _():
                t_copy(b, place).start()

        @pl.when(carried & (b == 0))
        def _():
            place = part_of(r)
            solved[0, :head] = -times(entering[:head], 1)
            add_up(place, times(solved[0, place], 2) + times(solved[1, place], 3))
            pair_even.start()
            carry_even[core] = solved[0, :head]

        @pl.when((b > 0) & (b < n_sum) & (spot < GROUP - 1))
        def _():
            place = data(b - 1)
            even = constants[0, place] - times(entering[place], 1)
            solved[0, place] = even
            add_up(place, times(even, 2) + times(solved[1, place], 3))

        @pl.when((b > 0) & (b < n_sum) & final)
        def _():
            place = data(b - 1)
            add_up(place, fixed[batch(b - 1)] + times(entering[place], 7))

        @pl.when(carried & final & (b == 0))
        def _():
            carry_sum[core, part_of(r)] = sums_out[part_of(r)]
            for shift in range(1, rows):
                k_copy(shift, part_of(r)).start()

        @pl.when(carried & final & (i == share_lag - 3))
        def _():
            received(carry_sum.at[core, pl.ds(0, (rows - 1) * piece)], k_recv.at[0])
            pair_sum.start()

        @pl.when(fills & (i == inflow_lag))
        def _():
            sent(entering, y_send)
            pair_carry.wait_recv()
            keep(4, carry[...].reshape(width, width))
            pair_even.wait_recv()
            keep(5, carry_even[...].reshape(width, width))

        @pl.when(carried & final & (i == inflow_lag))
        def _():
            pair_carry.wait_recv()
            keep(4, carry[...].reshape(width, width))

        m = i - inflow_lag

        @pl.when(carried & (m >= 0) & (m < n_data))
        def _():
            in_copy(m).wait_recv()

            @pl.when(relays & (first | jnp.logical_not(halved) | (m < n_data // 2)))
            def _():
                relay_copy(m).start()

            @pl.when(final & halved & jnp.logical_not(feeds) & (m >= n_data // 2))
            def _():
                back_copy(m).start()

            @pl.when(spot < GROUP - 1)
            def _():
                value = inflow[batch(m)]
                solved[1, data(m)] += times(value, 4)
                solved[0, data(m)] += times(value, 5)
                hand_in(m)

            @pl.when(final)
            def _():
                passed[batch(m)] = solved[1, data(m)] + times(inflow[batch(m)], 4)

            @pl.when(feeds)
            def _():
                in_copy(m).start()
                lead_copy(m).start()

        @pl.when(feeds & halved & (m == n_data))
        def _():
            def give_back(k, unused):
                back_copy(k).start()
                return unused

            lax.fori_loop(n_data // 2, n_data, give_back, 0)

        @pl.when(carried & final & (i == share_lag))
        def _():
            pair_sum.wait_recv()
            keep(6, carry_sum[...].reshape(width, width))

        t = i - share_lag

        @pl.when(final & (t >= 0) & (t < n_data // 2))
        def _():
            pair = pl.ds(pl.multiple_of(t * 2 * STEP, 2 * STEP), 2 * STEP)
            below = pl.ds(pl.multiple_of(t * 2 * STEP + head, 2 * STEP), 2 * STEP)

            @pl.when(carried)
            def _():
                share[pair] = sums_out[below] + times(inflow[pair], 6)

            @pl.when(group == 0)
            def _():
                share[pair] = sums_out[below]

            for b in (2 * t, 2 * t + 1):
                @pl.when(core * n_data + b != p)
                def _():
                    u_copy(b).start()

                @pl.when(core * n_data + b == p)
                def _():
                    total[group] = share[batch(b)]

        return unused

    lax.fori_loop(0, turns, turn, 0)

    @pl.when(final & carried)
    def _():
        solved[1, body] = passed[...]

    @pl.when(spot < GROUP - 1)
    def _():
        @pl.when(group == 0)
        def _():
            sent(entering.at[body], y_send)
            sent(sums_in.at[body], t_send)

        @pl.when(carried)
        def _():
            sent(sums_in.at[pl.ds(0, piece + half)], t_send)

    @pl.when(final)
    def _():
        solved[0, body] = constants[0, body] - times(entering[body], 1)

    @pl.when(final & carried)
    def _():
        pair_even.wait_recv()
        keep(5, carry_even[...].reshape(width, width))
        solved[0, body] += times(inflow[...], 5)

    @pl.when(jnp.logical_not(fills))
    def _():
        def hand_all(k, unused):
            hand_in(k)
            return unused

        lax.fori_loop(0, n_data, hand_all, 0)

    for k, start in enumerate(source_panels):
        @pl.when(start + side != p)
        def _():
            remote(share.at[batch(0)], total.at[k], u_send.at[0], u_recv.at[k], at(start + side)).wait_recv()

    local_cols.wait()
    summed = total[0]
    for k in range(1, groups):
        summed = summed + total[k]
    tail_ref[...] = cols[...] - summed

    received(factor_ref.at[mine], f_recv.at[0])
    sent(factor_ref.at[mine], f_send)

    @pl.when(feeds)
    def _():
        sent(inflow, in_send)
        sent(inflow, lead_send)

    part_relay = relays & halved & (spot > 0)

    @pl.when(relays & jnp.logical_not(part_relay))
    def _():
        sent(inflow, relay_send)

    @pl.when(part_relay)
    def _():
        sent(inflow.at[pl.ds(0, half // 2)], relay_send)

    @pl.when(halved & final)
    def _():
        sent(inflow.at[pl.ds(0, half // 2)], back_send)

    @pl.when(final & (side == core))
    def _():
        sent(share.at[pl.ds(0, half - STEP)], u_send)

    @pl.when(final & (side != core))
    def _():
        sent(share, u_send)

    sent(inverses.at[core, pl.ds(0, 2 * depth - 2)], z_send)
    sent(inverses.at[core], x_send)
    sent(couplings.at[core, pl.ds(0, rows - 1)], g_send)
    pair_slab.wait_send()
    pair_inverse.wait_send()
    pair_product.wait_send()
    pair_coupling.wait_send()

    @pl.when(carried)
    def _():
        pair_carry.wait_send()
        pair_even.wait_send()

    @pl.when(carried & final)
    def _():
        pair_sum.wait_send()
        sent(carry_sum.at[core, pl.ds(0, (rows - 1) * piece)], k_send)


def solution(mesh):
    panels, rows = mesh.shape["panel"], mesh.shape["row"]

    def on_device(slab, boundary, diag_inverse, sub_block, tail_coupling, tail_cols):
        height, width = slab.shape
        half, head = height // 2, width // 2
        extended = head + half
        depth = rows // 2
        n_data, n_all = half // STEP, extended // STEP
        groups = panels // 2 // GROUP
        f32, bf16 = jnp.float32, jnp.bfloat16
        shard = diag_inverse.shape[0]
        whole = pl.BlockSpec(memory_space=pltpu.VMEM)
        apart = pl.BlockSpec(memory_space=pltpu.HBM)
        dma = pltpu.SemaphoreType.DMA
        operands = [
            pltpu.with_memory_space_constraint(value, pltpu.HBM)
            for value in (slab, boundary, diag_inverse, sub_block, tail_coupling, tail_cols)
        ]
        return pl.pallas_call(
            functools.partial(kernel, panels, rows),
            out_shape=(
                jax.ShapeDtypeStruct((height, width), f32),
                jax.ShapeDtypeStruct(tail_cols.shape, f32),
            ),
            in_specs=[apart] * 6,
            out_specs=(whole, whole),
            scratch_shapes=[
                pltpu.VMEM((2, half, width), f32),
                pltpu.VMEM((2, rows, shard, width), f32),
                pltpu.VMEM((rows, shard, width), f32),
                pltpu.VMEM((2, rows, shard, width), f32),
                pltpu.VMEM((2, width, width), f32),
                pltpu.VMEM((2, extended, width), f32),
                pltpu.VMEM((extended, width), f32),
                pltpu.VMEM((extended, width), f32),
                pltpu.VMEM((2, extended, width), f32),
                pltpu.VMEM((extended, width), f32),
                pltpu.VMEM((extended, width), f32),
                pltpu.VMEM((half, width), f32),
                pltpu.VMEM((half, width), f32),
                pltpu.VMEM((2, head, width), f32),
                pltpu.VMEM((2, head, width), f32),
                pltpu.VMEM((2, head, width), f32),
                pltpu.VMEM((half, width), f32),
                pltpu.VMEM((8, width, width), bf16),
                pltpu.VMEM((8, width, width), bf16),
                pltpu.VMEM((half, width), f32),
                pltpu.VMEM((groups, STEP, width), f32),
                pltpu.VMEM(tail_cols.shape, f32),
                dma((1,)),
                dma((2, depth - 1)),
                dma((1,)),
                dma((2,)),
                dma((1,)),
                dma((1,)),
                dma((1,)),
                dma((1,)),
                dma((1,)),
                dma((1,)),
                dma((7,)),
                dma((7,)),
                dma((6,)),
                dma((1,)),
                dma((n_all,)),
                dma((1,)),
                dma((n_data + 1,)),
                dma((1,)),
                dma((n_data,)),
                dma((1,)),
                dma((1,)),
                dma((1,)),
                dma((1,)),
                dma((groups,)),
            ],
            compiler_params=pltpu.CompilerParams(
                collective_id=0, has_side_effects=True, vmem_limit_bytes=48 << 20
            ),
        )(*operands)

    placed = (
        P("row", "panel"),
        P("row", None),
        P(("panel", "row"), None),
        P(("panel", "row"), None),
        P(("panel", "row"), None),
        P(("row", "panel"), None),
    )
    return jax.shard_map(
        on_device,
        mesh=mesh,
        in_specs=placed,
        out_specs=(P("row", "panel"), P(("row", "panel"), None)),
        check_vma=False,
    )
```

```python
import functools

import jax
import jax.numpy as jnp
from jax import lax
from jax.experimental import pallas as pl
from jax.experimental.pallas import tpu as pltpu
from jax.sharding import PartitionSpec as P

MESH = pl.DeviceIdType.MESH
STEP = 32
GROUP = 4
NT = (((1,), (1,)), ((), ()))
NN = (((1,), (0,)), ((), ()))


def split(value):
    high = value.astype(jnp.bfloat16)
    low = (value - high.astype(jnp.float32)).astype(jnp.bfloat16)
    return high, low


def dot3(left, right, dims):
    left_high, left_low = split(left)
    right_high, right_low = split(right)
    dot = functools.partial(lax.dot_general, dimension_numbers=dims, preferred_element_type=jnp.float32)
    return dot(left_high, right_high) + (dot(left_high, right_low) + dot(left_low, right_high))


def kernel(
    panels, rows,
    slab, boundary, inverse_ref, beneath_ref, coupling_ref, cols_ref,
    factor_ref, tail_ref,
    slabs, inverses, beneath, couplings, products, constants, offset, entering, solved,
    sums_in, sums_out, inflow, passed, carry, carry_even, carry_sum, fixed, weight_high, weight_low, share, total, cols,
    z_send, z_recv, x_send, x_recv, g_send, g_recv, k_send, k_recv, f_send, f_recv, pair_send, pair_recv, local_sem,
    y_send, y_recv, t_send, t_recv, in_send, in_recv, lead_send, relay_send, back_send, u_send, u_recv,
):
    p, r = lax.axis_index("panel"), lax.axis_index("row")
    core = lax.rem(p, 2)
    chip = lax.div(p, 2)
    chips = panels // 2
    groups = chips // GROUP
    group, spot = lax.div(chip, GROUP), lax.rem(chip, GROUP)
    side = lax.div(p, panels // 2)
    z, x = lax.div(r, 2), lax.rem(r, 2)
    depth = rows // 2
    half = slab.shape[0] // 2
    width = slab.shape[1]
    head = width // 2
    n_head, n_data = head // STEP, half // STEP
    n_all = n_head + n_data
    n_sum = 1 + n_data
    piece = head // rows
    body = pl.ds(head, half)
    mine = pl.ds(pl.multiple_of(core * half, half), half)
    other = pl.ds(pl.multiple_of((1 - core) * half, half), half)
    steps = sorted(range(1, depth), key=lambda d: (-min(d, depth - d), d))

    first, final = spot == 0, spot == GROUP - 1
    carried = group > 0
    feeds = final & (group < groups - 1)
    halved = group == 1

    def at(panel):
        return {"panel": panel, "row": r}

    sibling = at(p + 1 - 2 * core)
    beside = {"panel": p, "row": r + 1 - 2 * x}
    after, ahead = at(p + 2), at(p - 2)
    skip_after, skip_ahead = at(p + 2 * GROUP), at(p - 2 * GROUP)
    source_panels = [2 * (GROUP * k + GROUP - 1) for k in range(groups)]

    def z_row(shift):
        return lax.rem(z + shift + depth, depth) * 2 + x

    def any_row(shift):
        return lax.rem(r + shift + rows, rows)

    barrier = pltpu.get_barrier_semaphore()

    def greet(target):
        pl.semaphore_signal(barrier, inc=1, device_id=target, device_id_type=MESH)

    for shift in range(1, rows):
        greet({"panel": p, "row": any_row(shift)})
    greet(sibling)

    @pl.when(chip > 0)
    def _():
        greet(ahead)

    @pl.when(halved & (spot == GROUP - 2))
    def _():
        greet(after)

    @pl.when(final & carried)
    def _():
        greet(skip_ahead)

    for start in source_panels:
        @pl.when(start + side != p)
        def _():
            greet(at(start + side))

    local_slab = pltpu.make_async_copy(slab.at[mine], slabs.at[core], local_sem.at[0])
    local_slab.start()
    local_cols = pltpu.make_async_copy(cols_ref, cols, local_sem.at[1])
    local_cols.start()
    local_boundary = pltpu.make_async_copy(boundary.at[mine], entering.at[body], local_sem.at[2])

    @pl.when(chip == 0)
    def _():
        local_boundary.start()

    full = (inverses.at[core], beneath, couplings.at[core])
    shards = (inverse_ref, beneath_ref, coupling_ref)
    local_shards = [pltpu.make_async_copy(shards[k], full[k].at[r], local_sem.at[3 + k]) for k in range(3)]
    for copy in local_shards:
        copy.start()

    expected = (
        rows + jnp.where(chip < chips - 1, 1, 0) + jnp.where(feeds, 1, 0) + jnp.where(halved & final, 1, 0)
        + jnp.where(final, jnp.where(side == core, n_data - 1, n_data), 0)
    )
    pl.semaphore_wait(barrier, expected)

    def remote(src, dst, send, recv, target):
        return pltpu.make_async_remote_copy(
            src_ref=src, dst_ref=dst, send_sem=send, recv_sem=recv, device_id=target, device_id_type=MESH
        )

    def z_copy(k, i, shift, place):
        return remote(
            shards[k], full[k].at[place], z_send.at[0], z_recv.at[k, i], {"panel": p, "row": z_row(shift)}
        )

    def x_own(k):
        return remote(shards[k], full[k].at[r], x_send.at[0], x_recv.at[k], beside)

    def x_relay(k, i, shift):
        place = full[k].at[z_row(-shift)]
        return remote(place, place, x_send.at[0], x_recv.at[k], beside)

    def g_copy(shift, place):
        return remote(
            shards[2], full[2].at[place], g_send.at[0], g_recv.at[0],
            {"panel": p, "row": any_row(shift)},
        )

    def to_sibling(k, src, dst):
        return remote(src, dst, pair_send.at[k], pair_recv.at[k], sibling)

    pair_slab = to_sibling(0, slab.at[other], slabs.at[core])
    pair_inverse = to_sibling(1, inverses.at[core], inverses.at[core])
    pair_product = to_sibling(2, products.at[core], products.at[core])
    pair_coupling = to_sibling(3, couplings.at[core], couplings.at[core])
    pair_carry = to_sibling(4, solved.at[1, pl.ds(0, head)], carry.at[core])
    pair_even = to_sibling(5, solved.at[0, pl.ds(0, head)], carry_even.at[core])
    pair_sum = to_sibling(6, carry_sum.at[core], carry_sum.at[core])

    for k in range(2):
        x_own(k).start()
        for i, shift in enumerate(steps):
            z_copy(k, i, shift, r).start()
        if k == 0:
            pair_slab.start()
    for copy in local_shards:
        copy.wait()

    def relay(k):
        for i, shift in enumerate(steps):
            z_copy(k, i, shift, z_row(-shift)).wait_recv()
            x_relay(k, i, shift).start()

    def sent(ref, sem):
        remote(ref, ref, sem.at[0], sem.at[0], sibling).wait_send()

    def received(ref, sem):
        remote(ref, ref, sem, sem, sibling).wait_recv()

    def x_arrivals(k):
        received(full[k].at[pl.ds(0, depth)], x_recv.at[k])

    def square(ref):
        return ref[...].reshape(width, width)

    def keep(k, value):
        weight_high[k], weight_low[k] = split(value)

    def times(value, k):
        high, low = split(value)
        count = value.shape[0]
        both = jnp.dot(jnp.concatenate([high, low], axis=0), weight_high[k], preferred_element_type=jnp.float32)
        rest = jnp.dot(high, weight_low[k], preferred_element_type=jnp.float32)
        return both[:count] + (both[count:] + rest)

    zeros = jnp.zeros((head, width), jnp.float32)
    offset[:head] = zeros
    constants[0, :head] = zeros

    @pl.when(first)
    def _():
        row = lax.broadcasted_iota(jnp.int32, (head, width), 0) + core * head
        column = lax.broadcasted_iota(jnp.int32, (head, width), 1)
        entering[:head] = jnp.where(row == column, 1.0, 0.0)

    @pl.when(first & carried)
    def _():
        entering[body] = jnp.zeros((half, width), jnp.float32)

    relay(0)
    relay(1)
    x_arrivals(0)
    pair_inverse.start()
    local_slab.wait()
    constants[core, body] = dot3(slabs[core], square(inverses.at[core]), NT)
    pair_slab.wait_recv()
    pair_inverse.wait_recv()
    constants[1 - core, body] = dot3(slabs[1 - core], square(inverses.at[1 - core]), NT)
    x_arrivals(1)
    products[core] = dot3(square(inverses.at[core]), square(beneath), NN)
    pair_product.start()
    for shift in range(1, rows):
        g_copy(shift, r).start()
    pair_product.wait_recv()
    keep(0, dot3(products[1], products[0], NN).T)
    offset[body] = constants[1, body] - dot3(constants[0, body], products[1], NT)

    @pl.when(chip == 0)
    def _():
        local_boundary.wait()

    def batch(b):
        return pl.ds(pl.multiple_of(b * STEP, STEP), STEP)

    def data(b):
        return pl.ds(pl.multiple_of(b * STEP + head, STEP), STEP)

    def y_copy(b):
        return remote(solved.at[1, batch(b)], entering.at[batch(b)], y_send.at[0], y_recv.at[b], after)

    def part_of(row):
        return pl.ds(pl.multiple_of(row * piece, piece), piece)

    def t_copy(b, place):
        return remote(sums_out.at[place], sums_in.at[place], t_send.at[0], t_recv.at[b], after)

    def k_copy(shift, place):
        return remote(
            sums_out.at[part_of(r)], carry_sum.at[core, place], k_send.at[0], k_recv.at[0],
            {"panel": p, "row": any_row(shift)},
        )

    def factor_copy(b):
        place = pl.ds(pl.multiple_of(core * half + b * STEP, STEP), STEP)
        return remote(solved.at[1 - core, data(b)], factor_ref.at[place], f_send.at[0], f_recv.at[0], sibling)

    def hand_in(b):
        place = pl.ds(pl.multiple_of(core * half + b * STEP, STEP), STEP)
        factor_copy(b).start()
        factor_ref[place] = solved[core, data(b)]

    def in_copy(b):
        return remote(passed.at[batch(b)], inflow.at[batch(b)], in_send.at[0], in_recv.at[b], skip_after)

    def lead_copy(b):
        return remote(passed.at[batch(b)], inflow.at[batch(b)], lead_send.at[0], in_recv.at[b], after)

    def relay_copy(b):
        return remote(inflow.at[batch(b)], inflow.at[batch(b)], relay_send.at[0], in_recv.at[b], after)

    def back_copy(b):
        return remote(inflow.at[batch(b)], inflow.at[batch(b)], back_send.at[0], in_recv.at[b], ahead)

    def u_copy(b):
        return remote(
            share.at[batch(b)], total.at[group], u_send.at[0], u_recv.at[group], at(core * n_data + b)
        )

    begin = jnp.where(carried, 0, n_head)
    couple_turn = jnp.where(final, 8, n_all - 4)
    fix_turn = jnp.where(final, 12, n_all)
    relays = carried & (spot < GROUP - 2)
    fills = carried & (spot < GROUP - 1)
    inflow_lag = jnp.where(final, 8 * group, n_all + n_sum + 1)
    sum_lag = n_all
    share_lag = jnp.where(carried, sum_lag + 13, sum_lag + 9)
    turns = n_all + n_sum + 1 + n_data

    def turn(i, unused):
        @pl.when((i >= begin) & (i < n_all))
        def _():
            @pl.when(spot > 0)
            def _():
                y_copy(i).wait_recv()

            row = offset[batch(i)] + times(entering[batch(i)], 0)
            solved[1, batch(i)] = row

            @pl.when(spot < GROUP - 1)
            def _():
                y_copy(i).start()

            @pl.when(final & (group == 0))
            def _():
                passed[batch(i - n_head)] = row
                in_copy(i - n_head).start()
                lead_copy(i - n_head).start()

        @pl.when(carried & (i == n_head))
        def _():
            pair_carry.start()
            carry[core] = solved[1, :head]

        @pl.when(i == couple_turn)
        def _():
            received(couplings.at[core, pl.ds(0, rows - 1)], g_recv.at[0])
            pair_coupling.start()

        @pl.when(i == fix_turn)
        def _():
            pair_coupling.wait_recv()
            keep(1, products[0].T)
            keep(2, square(couplings.at[0]))
            keep(3, square(couplings.at[1]))

        @pl.when(final & (i == fix_turn))
        def _():
            step = weight_high[0].astype(jnp.float32) + weight_low[0].astype(jnp.float32)
            keep(7, times(step, 3) - times(products[0].T, 2))
            fixed[...] = times(constants[0, body], 2) + times(offset[body], 3)

        b = i - sum_lag

        def add_up(place, part):
            @pl.when(first)
            def _():
                sums_out[place] = part

            @pl.when(spot > 0)
            def _():
                t_copy(b, place).wait_recv()
                sums_out[place] = sums_in[place] + part

            @pl.when(spot < GROUP - 1)
            def _():
                t_copy(b, place).start()

        @pl.when(carried & (b == 0))
        def _():
            place = part_of(r)
            solved[0, :head] = -times(entering[:head], 1)
            add_up(place, times(solved[0, place], 2) + times(solved[1, place], 3))
            pair_even.start()
            carry_even[core] = solved[0, :head]

        @pl.when((b > 0) & (b < n_sum) & (spot < GROUP - 1))
        def _():
            place = data(b - 1)
            even = constants[0, place] - times(entering[place], 1)
            solved[0, place] = even
            add_up(place, times(even, 2) + times(solved[1, place], 3))

        @pl.when((b > 0) & (b < n_sum) & final)
        def _():
            place = data(b - 1)
            add_up(place, fixed[batch(b - 1)] + times(entering[place], 7))

        @pl.when(carried & final & (b == 0))
        def _():
            carry_sum[core, part_of(r)] = sums_out[part_of(r)]
            for shift in range(1, rows):
                k_copy(shift, part_of(r)).start()

        @pl.when(carried & final & (i == share_lag - 3))
        def _():
            received(carry_sum.at[core, pl.ds(0, (rows - 1) * piece)], k_recv.at[0])
            pair_sum.start()

        @pl.when(fills & (i == inflow_lag))
        def _():
            sent(entering, y_send)
            pair_carry.wait_recv()
            keep(4, carry[...].reshape(width, width))
            pair_even.wait_recv()
            keep(5, carry_even[...].reshape(width, width))

        @pl.when(carried & final & (i == inflow_lag))
        def _():
            pair_carry.wait_recv()
            keep(4, carry[...].reshape(width, width))

        m = i - inflow_lag

        @pl.when(carried & (m >= 0) & (m < n_data))
        def _():
            in_copy(m).wait_recv()

            @pl.when(relays & (first | jnp.logical_not(halved) | (m < n_data // 2)))
            def _():
                relay_copy(m).start()

            @pl.when(final & halved & jnp.logical_not(feeds) & (m >= n_data // 2))
            def _():
                back_copy(m).start()

            @pl.when(spot < GROUP - 1)
            def _():
                value = inflow[batch(m)]
                solved[1, data(m)] += times(value, 4)
                solved[0, data(m)] += times(value, 5)
                hand_in(m)

            @pl.when(final)
            def _():
                passed[batch(m)] = solved[1, data(m)] + times(inflow[batch(m)], 4)

            @pl.when(feeds)
            def _():
                in_copy(m).start()
                lead_copy(m).start()

        @pl.when(feeds & halved & (m == n_data))
        def _():
            def give_back(k, unused):
                back_copy(k).start()
                return unused

            lax.fori_loop(n_data // 2, n_data, give_back, 0)

        @pl.when(carried & final & (i == share_lag))
        def _():
            pair_sum.wait_recv()
            keep(6, carry_sum[...].reshape(width, width))

        t = i - share_lag

        @pl.when(final & (t >= 0) & (t < n_data // 2))
        def _():
            pair = pl.ds(pl.multiple_of(t * 2 * STEP, 2 * STEP), 2 * STEP)
            below = pl.ds(pl.multiple_of(t * 2 * STEP + head, 2 * STEP), 2 * STEP)

            @pl.when(carried)
            def _():
                share[pair] = sums_out[below] + times(inflow[pair], 6)

            @pl.when(group == 0)
            def _():
                share[pair] = sums_out[below]

            for b in (2 * t, 2 * t + 1):
                @pl.when(core * n_data + b != p)
                def _():
                    u_copy(b).start()

                @pl.when(core * n_data + b == p)
                def _():
                    total[group] = share[batch(b)]

        return unused

    lax.fori_loop(0, turns, turn, 0)

    @pl.when(final & carried)
    def _():
        solved[1, body] = passed[...]

    @pl.when(spot < GROUP - 1)
    def _():
        @pl.when(group == 0)
        def _():
            sent(entering.at[body], y_send)
            sent(sums_in.at[body], t_send)

        @pl.when(carried)
        def _():
            sent(sums_in.at[pl.ds(0, piece + half)], t_send)

    @pl.when(final)
    def _():
        solved[0, body] = constants[0, body] - times(entering[body], 1)

    @pl.when(final & carried)
    def _():
        pair_even.wait_recv()
        keep(5, carry_even[...].reshape(width, width))
        solved[0, body] += times(inflow[...], 5)

    @pl.when(jnp.logical_not(fills))
    def _():
        def hand_all(k, unused):
            hand_in(k)
            return unused

        lax.fori_loop(0, n_data, hand_all, 0)

    for k, start in enumerate(source_panels):
        @pl.when(start + side != p)
        def _():
            remote(share.at[batch(0)], total.at[k], u_send.at[0], u_recv.at[k], at(start + side)).wait_recv()

    local_cols.wait()
    summed = total[0]
    for k in range(1, groups):
        summed = summed + total[k]
    tail_ref[...] = cols[...] - summed

    received(factor_ref.at[mine], f_recv.at[0])
    sent(factor_ref.at[mine], f_send)

    @pl.when(feeds)
    def _():
        sent(inflow, in_send)
        sent(inflow, lead_send)

    part_relay = relays & halved & (spot > 0)

    @pl.when(relays & jnp.logical_not(part_relay))
    def _():
        sent(inflow, relay_send)

    @pl.when(part_relay)
    def _():
        sent(inflow.at[pl.ds(0, half // 2)], relay_send)

    @pl.when(halved & final)
    def _():
        sent(inflow.at[pl.ds(0, half // 2)], back_send)

    @pl.when(final & (side == core))
    def _():
        sent(share.at[pl.ds(0, half - STEP)], u_send)

    @pl.when(final & (side != core))
    def _():
        sent(share, u_send)

    sent(inverses.at[core, pl.ds(0, 2 * depth - 2)], z_send)
    sent(inverses.at[core], x_send)
    sent(couplings.at[core, pl.ds(0, rows - 1)], g_send)
    pair_slab.wait_send()
    pair_inverse.wait_send()
    pair_product.wait_send()
    pair_coupling.wait_send()

    @pl.when(carried)
    def _():
        pair_carry.wait_send()
        pair_even.wait_send()

    @pl.when(carried & final)
    def _():
        pair_sum.wait_send()
        sent(carry_sum.at[core, pl.ds(0, (rows - 1) * piece)], k_send)


def solution(mesh):
    panels, rows = mesh.shape["panel"], mesh.shape["row"]

    def on_device(slab, boundary, diag_inverse, sub_block, tail_coupling, tail_cols):
        height, width = slab.shape
        half, head = height // 2, width // 2
        extended = head + half
        depth = rows // 2
        n_data, n_all = half // STEP, extended // STEP
        groups = panels // 2 // GROUP
        f32, bf16 = jnp.float32, jnp.bfloat16
        shard = diag_inverse.shape[0]
        whole = pl.BlockSpec(memory_space=pltpu.VMEM)
        apart = pl.BlockSpec(memory_space=pltpu.HBM)
        dma = pltpu.SemaphoreType.DMA
        operands = [
            pltpu.with_memory_space_constraint(value, pltpu.HBM)
            for value in (slab, boundary, diag_inverse, sub_block, tail_coupling, tail_cols)
        ]
        return pl.pallas_call(
            functools.partial(kernel, panels, rows),
            out_shape=(
                jax.ShapeDtypeStruct((height, width), f32),
                jax.ShapeDtypeStruct(tail_cols.shape, f32),
            ),
            in_specs=[apart] * 6,
            out_specs=(whole, whole),
            scratch_shapes=[
                pltpu.VMEM((2, half, width), f32),
                pltpu.VMEM((2, rows, shard, width), f32),
                pltpu.VMEM((rows, shard, width), f32),
                pltpu.VMEM((2, rows, shard, width), f32),
                pltpu.VMEM((2, width, width), f32),
                pltpu.VMEM((2, extended, width), f32),
                pltpu.VMEM((extended, width), f32),
                pltpu.VMEM((extended, width), f32),
                pltpu.VMEM((2, extended, width), f32),
                pltpu.VMEM((extended, width), f32),
                pltpu.VMEM((extended, width), f32),
                pltpu.VMEM((half, width), f32),
                pltpu.VMEM((half, width), f32),
                pltpu.VMEM((2, head, width), f32),
                pltpu.VMEM((2, head, width), f32),
                pltpu.VMEM((2, head, width), f32),
                pltpu.VMEM((half, width), f32),
                pltpu.VMEM((8, width, width), bf16),
                pltpu.VMEM((8, width, width), bf16),
                pltpu.VMEM((half, width), f32),
                pltpu.VMEM((groups, STEP, width), f32),
                pltpu.VMEM(tail_cols.shape, f32),
                dma((1,)),
                dma((2, depth - 1)),
                dma((1,)),
                dma((2,)),
                dma((1,)),
                dma((1,)),
                dma((1,)),
                dma((1,)),
                dma((1,)),
                dma((1,)),
                dma((7,)),
                dma((7,)),
                dma((6,)),
                dma((1,)),
                dma((n_all,)),
                dma((1,)),
                dma((n_data + 1,)),
                dma((1,)),
                dma((n_data,)),
                dma((1,)),
                dma((1,)),
                dma((1,)),
                dma((1,)),
                dma((groups,)),
            ],
            compiler_params=pltpu.CompilerParams(
                collective_id=0, has_side_effects=True, vmem_limit_bytes=48 << 20
            ),
        )(*operands)

    placed = (
        P("row", "panel"),
        P("row", None),
        P(("panel", "row"), None),
        P(("panel", "row"), None),
        P(("panel", "row"), None),
        P(("row", "panel"), None),
    )
    return jax.shard_map(
        on_device,
        mesh=mesh,
        in_specs=placed,
        out_specs=(P("row", "panel"), P(("row", "panel"), None)),
        check_vma=False,
    )
```
